32 devices in a mesh: seq: 16 (over z, x, core), head: 2 (over y).
Axes of the slice: x: 2, y: 2, z: 4, core: 2. Of those that a mesh axis runs over, the one named last changes fastest.
Arguments:
- query: bfloat16 [2048, 8192], P(('seq', 'head')), may hold values from -6 to 6
- key: bfloat16 [2048, 8192], P(('seq', 'head')), may hold values from -6 to 6
- value: bfloat16 [2048, 8192], P(('seq', 'head')), may hold values from -6 to 6
- cotangent: bfloat16 [2048, 8192], P(('seq', 'head')), may hold values from -6 to 6
- gain: float32 [8192], P('head'), may hold values from 0.5 to 1.5
- incoming_state: float32 [64, 128, 128], P('head'), may hold values from -288 to 288
Outputs:
- output: bfloat16 [2048, 8192], P(('seq', 'head'))
- grad_query: bfloat16 [2048, 8192], P(('seq', 'head'))
- grad_key: bfloat16 [2048, 8192], P(('seq', 'head'))
- grad_value: bfloat16 [2048, 8192], P(('seq', 'head'))
The draws below stay inside these ranges and needn't reach their ends.
All inputs are finite; a program needn't handle non-finite values.
Results may differ from the reference program's by a relative error of at most 0.0058.
Values may be sent and summed in bfloat16 or wider, within the bound.
A program may use at most 128 MiB of HBM per device.

```python
import jax
import jax.numpy as jnp
from jax import lax

HEADS = 64
HEAD_DIM = 128
TOK_DEV = 128
WIDTH = 8192
TOKENS = 2048
N_SEQ = 16


def block_scale(own_key, dims, cuts, smallest, high):
    level = 1.0
    for axis_at, shards_of in cuts:
        heights = jax.random.uniform(jax.random.fold_in(jax.random.fold_in(own_key, 6), axis_at), (shards_of,), jnp.float32, smallest / len(cuts), high / len(cuts))
        level = level * jnp.repeat(jnp.exp(heights), dims[axis_at] // shards_of).reshape((-1,) + (1,) * (len(dims) - 1 - axis_at))
    return level


def centred(own_key, dims, width, limit, split=(), kind=jnp.bfloat16):
    result = jax.random.normal(own_key, dims, jnp.float32) * width
    if len(split) > 0:
        result = block_scale(own_key, dims, split, -0.22, 0.18) * result
    return jnp.clip(result, min=-limit, max=limit).astype(kind)


def setup_inputs(seed: int = 0) -> dict:
    splits = jax.random.split(jax.random.key(seed), 7)
    return {
        "query": centred(splits[0], (TOKENS, WIDTH), 1.0, 6.0, ((0, 32),)),
        "key": centred(splits[1], (TOKENS, WIDTH), 1.0, 6.0, ((0, 32),)),
        "value": centred(splits[2], (TOKENS, WIDTH), 1.0, 6.0, ((0, 32),)),
        "cotangent": centred(splits[3], (TOKENS, WIDTH), 1.0, 6.0, ((0, 32),)),
        "gain": jnp.clip(1.0 + 0.1 * jax.random.normal(splits[4], (WIDTH,), jnp.float32), 0.5, 1.5),
        "incoming_state": centred(splits[5], (HEADS, HEAD_DIM, HEAD_DIM), 48.0, 288.0, ((0, 2),), jnp.float32),
    }


EPSILON = 1e-06

def head_pass(packed):
    query_block, key_block, value_block, upstream, gain_row, carried = packed
    causal = jnp.tril(jnp.ones((TOK_DEV, TOK_DEV), dtype=bool))
    query_wide = query_block.astype(jnp.float32)
    key_wide = key_block.astype(jnp.float32)
    value_wide = value_block.astype(jnp.float32)
    scores = jnp.einsum('ctd,csd->cts', query_wide, key_wide)
    weights = jnp.where(causal, scores, 0.0).astype(jnp.bfloat16)
    weights_wide = weights.astype(jnp.float32)
    within = jnp.einsum('cts,cse->cte', weights_wide, value_wide)
    block_state = jnp.einsum('csd,cse->cde', key_wide, value_wide)
    prefix = jnp.cumsum(block_state, axis=0) - block_state + carried[None]
    states = prefix.astype(jnp.bfloat16).astype(jnp.float32)
    attention = within + jnp.einsum('ctd,cde->cte', query_wide, states)
    root_mean = jnp.sqrt(lax.optimization_barrier(jnp.mean(attention * attention, axis=-1, keepdims=True)) + EPSILON)
    normed = attention / root_mean
    output = (normed * gain_row).astype(jnp.bfloat16)
    scaled = upstream.astype(jnp.float32) * gain_row
    grad_attn = ((scaled - normed * lax.optimization_barrier(jnp.mean(scaled * normed, axis=-1, keepdims=True))) / root_mean).astype(jnp.bfloat16)
    grad_wide = grad_attn.astype(jnp.float32)
    grad_scores = jnp.where(causal, jnp.einsum('cte,cse->cts', grad_wide, value_wide), 0.0).astype(jnp.bfloat16)
    grad_scores_wide = grad_scores.astype(jnp.float32)
    grad_state = jnp.einsum('ctd,cte->cde', query_wide, grad_wide)
    suffix = jnp.cumsum(grad_state[::-1], axis=0)[::-1] - grad_state
    later_states = suffix.astype(jnp.bfloat16).astype(jnp.float32)
    grad_query = jnp.einsum('cts,csd->ctd', grad_scores_wide, key_wide) + jnp.einsum('cte,cde->ctd', grad_wide, states)
    grad_key = jnp.einsum('cts,ctd->csd', grad_scores_wide, query_wide) + jnp.einsum('cse,cde->csd', value_wide, later_states)
    grad_value = jnp.einsum('cts,cte->cse', weights_wide, grad_wide) + jnp.einsum('csd,cde->cse', key_wide, later_states)
    return (output, grad_query.astype(jnp.bfloat16), grad_key.astype(jnp.bfloat16), grad_value.astype(jnp.bfloat16))

def split_heads(array):
    return array.reshape(N_SEQ, TOK_DEV, HEADS, HEAD_DIM).transpose(2, 0, 1, 3)

def join_heads(array):
    return array.transpose(1, 2, 0, 3).reshape(TOKENS, HEADS * HEAD_DIM)

def reference(query, key, value, cotangent, gain, incoming_state):
    packed = (split_heads(query), split_heads(key), split_heads(value), split_heads(cotangent), gain.reshape(HEADS, 1, 1, HEAD_DIM), incoming_state)
    results = lax.map(head_pass, packed)
    return (join_heads(results[0]), join_heads(results[1]), join_heads(results[2]), join_heads(results[3]))
```

```python
import functools

import jax
import jax.numpy as jnp
from jax import lax
from jax.experimental import pallas as pl
from jax.experimental.pallas import tpu as pltpu
from jax.sharding import PartitionSpec as P

HEAD_DIM = 128
EPSILON = 1e-06
MESH = pl.DeviceIdType.MESH
F32 = jnp.float32
BF16 = jnp.bfloat16

NT = (((1,), (1,)), ((), ()))
TN = (((0,), (0,)), ((), ()))
NN = (((1,), (0,)), ((), ()))


def dot(a, b, dims):
    return lax.dot_general(a, b, dims, preferred_element_type=F32)


def kernel(plan, q_hbm, k_hbm, v_hbm, y_hbm, gain_hbm, s0_hbm, o_hbm, gq_hbm, gk_hbm, gv_hbm,
           xin, xout, part, cum, gcum, pin, psend, sin, ssend, tot, gain,
           in_send, in_recv, out_send, out_recv, p_send, p_recv, s_send, s_recv, gain_sem):
    n_groups, sub, n_head, rows, heads, step = plan
    peers = sub * n_head
    chunks = heads // step
    block = rows * n_head
    width = heads * HEAD_DIM
    span = step * HEAD_DIM
    seq, hd = lax.axis_index("seq"), lax.axis_index("head")
    group, j = seq // sub, lax.rem(seq, sub)
    me = j * n_head + hd

    def place(p):
        other = lax.rem(me + p, peers)
        return other, (group * sub + other // n_head, lax.rem(other, n_head))

    def column(other, c):
        owner = lax.rem(other, n_head) * (sub * heads) + (other // n_head) * heads + c * step
        return pl.ds(pl.multiple_of(owner * HEAD_DIM, span), span)

    def strip(index):
        return pl.ds(pl.multiple_of(index * rows, rows), rows)

    later = (seq + sub, hd)
    earlier = (seq - sub, hd)
    barrier = pltpu.get_barrier_semaphore()

    def greet(p, carry):
        _, device = place(p)
        pl.semaphore_signal(barrier, inc=1, device_id=device, device_id_type=MESH)
        return carry

    lax.fori_loop(1, peers, greet, 0)

    @pl.when(group > 0)
    def _():
        pl.semaphore_signal(barrier, inc=1, device_id=earlier, device_id_type=MESH)

    @pl.when(group < n_groups - 1)
    def _():
        pl.semaphore_signal(barrier, inc=1, device_id=later, device_id_type=MESH)

    sources = ((k_hbm, v_hbm), (q_hbm, y_hbm))
    targets = ((o_hbm, gq_hbm), (gk_hbm, gv_hbm))

    for phase in range(2):
        for c in range(chunks):
            cols = pl.ds(c * span, span)
            for a in range(2):
                pltpu.make_async_copy(
                    sources[phase][a].at[:, column(me, c)],
                    xin.at[2 * phase + a, strip(me), cols],
                    in_recv.at[phase, c],
                ).start()

    gains = pltpu.make_async_copy(gain_hbm, gain, gain_sem)
    gains.start()

    @pl.when(group == 0)
    def _():
        for c in range(chunks):
            pltpu.make_async_copy(
                s0_hbm.at[pl.ds(j * heads + c * step, step)],
                pin.at[pl.ds(c * step, step)],
                p_recv.at[c],
            ).start()

    if n_groups == 1:
        pl.semaphore_wait(barrier, peers - 1)
    else:
        inner = jnp.logical_and(group > 0, group < n_groups - 1)

        @pl.when(inner)
        def _():
            pl.semaphore_wait(barrier, peers + 1)

        @pl.when(jnp.logical_not(inner))
        def _():
            pl.semaphore_wait(barrier, peers)

    for phase in range(2):
        for c in range(chunks):
            cols = pl.ds(c * span, span)

            def scatter(p, carry, phase=phase, c=c, cols=cols):
                other, device = place(p)
                for a in range(2):
                    pltpu.make_async_remote_copy(
                        src_ref=sources[phase][a].at[:, column(other, c)],
                        dst_ref=xin.at[2 * phase + a, strip(me), cols],
                        send_sem=in_send.at[phase, c],
                        recv_sem=in_recv.at[phase, c],
                        device_id=device,
                        device_id_type=MESH,
                    ).start()
                return carry

            lax.fori_loop(1, peers, scatter, 0)

    def arrived(phase, c):
        ref = xin.at[pl.ds(2 * phase, 2), :, pl.ds(c * span, span)]
        pltpu.make_async_copy(ref, ref, in_recv.at[phase, c]).wait()

    def give(phase, c):
        cols = pl.ds(c * span, span)

        def back(p, carry):
            other, device = place(p)
            for a in range(2):
                pltpu.make_async_remote_copy(
                    src_ref=xout.at[2 * phase + a, strip(other), cols],
                    dst_ref=targets[phase][a].at[:, column(me, c)],
                    send_sem=out_send.at[phase, c],
                    recv_sem=out_recv.at[phase, c],
                    device_id=device,
                    device_id_type=MESH,
                ).start()
            return carry

        lax.fori_loop(1, peers, back, 0)
        for a in range(2):
            pltpu.make_async_copy(
                xout.at[2 * phase + a, strip(me), cols],
                targets[phase][a].at[:, column(me, c)],
                out_recv.at[phase, c],
            ).start()

    def state_copy(src, dst, send, recv, c, device):
        piece = pl.ds(c * step, step)
        return pltpu.make_async_remote_copy(
            src_ref=src.at[piece], dst_ref=dst.at[piece], send_sem=send.at[c],
            recv_sem=recv.at[c], device_id=device, device_id_type=MESH)

    def pass_prefix(c):
        piece = pl.ds(c * step, step)
        pltpu.make_async_copy(pin.at[piece], pin.at[piece], p_recv.at[c]).wait()

        @pl.when(group < n_groups - 1)
        def _():
            psend[c * step:(c + 1) * step] = (
                pin[c * step:(c + 1) * step] + tot[c * step:(c + 1) * step])
            state_copy(psend, pin, p_send, p_recv, c, later).start()

    for c in range(chunks):
        arrived(0, c)
        for h in range(c * step, (c + 1) * step):
            hc = slice(h * HEAD_DIM, (h + 1) * HEAD_DIM)
            run = jnp.zeros((HEAD_DIM, HEAD_DIM), F32)
            for b in range(sub):
                r = slice(b * block, (b + 1) * block)
                cum[h, b] = run
                run = run + dot(xin[0, r, hc], xin[1, r, hc], TN)
            tot[h] = run

        @pl.when(group == 0)
        def _(c=c):
            pass_prefix(c)

    row = lax.broadcasted_iota(jnp.int32, (block, block), 0)
    col = lax.broadcasted_iota(jnp.int32, (block, block), 1)
    causal = col <= row
    gains.wait()

    for c in range(chunks):
        @pl.when(group > 0)
        def _(c=c):
            pass_prefix(c)

    for c in range(chunks):
        arrived(1, c)
        for h in range(c * step, (c + 1) * step):
            hc = slice(h * HEAD_DIM, (h + 1) * HEAD_DIM)
            g = gain[pl.ds(j * heads + h, 1), :]
            carried = pin[h]
            run = jnp.zeros((HEAD_DIM, HEAD_DIM), F32)
            for b in reversed(range(sub)):
                r = slice(b * block, (b + 1) * block)
                k, v, q, up = xin[0, r, hc], xin[1, r, hc], xin[2, r, hc], xin[3, r, hc]
                state = (carried + cum[h, b]).astype(BF16)
                w = jnp.where(causal, dot(q, k, NT), 0.0).astype(BF16)
                att = dot(w, v, NN) + dot(q, state, NN)
                inv = lax.rsqrt(jnp.mean(att * att, axis=-1, keepdims=True) + EPSILON)
                normed = att * inv
                xout[0, r, hc] = (normed * g).astype(BF16)
                scaled = up.astype(F32) * g
                ga = ((scaled - normed * jnp.mean(scaled * normed, axis=-1, keepdims=True))
                      * inv).astype(BF16)
                gw = jnp.where(causal, dot(ga, v, NT), 0.0).astype(BF16)
                xout[1, r, hc] = (dot(gw, k, NN) + dot(ga, state, NT)).astype(BF16)
                part[0, r, hc] = dot(gw, q, TN)
                part[1, r, hc] = dot(w, ga, TN)
                gcum[h, b] = run
                run = run + dot(q, ga, TN)
            tot[h] = run

        @pl.when(jnp.logical_and(group == n_groups - 1, group > 0))
        def _(c=c):
            ssend[c * step:(c + 1) * step] = tot[c * step:(c + 1) * step]
            state_copy(ssend, sin, s_send, s_recv, c, earlier).start()

        give(0, c)

    for c in range(chunks):
        piece = pl.ds(c * step, step)

        @pl.when(group == n_groups - 1)
        def _(c=c):
            sin[c * step:(c + 1) * step] = jnp.zeros((step, HEAD_DIM, HEAD_DIM), F32)

        @pl.when(group < n_groups - 1)
        def _(c=c, piece=piece):
            pltpu.make_async_copy(sin.at[piece], sin.at[piece], s_recv.at[c]).wait()

            @pl.when(group > 0)
            def _():
                ssend[c * step:(c + 1) * step] = (
                    sin[c * step:(c + 1) * step] + tot[c * step:(c + 1) * step])
                state_copy(ssend, sin, s_send, s_recv, c, earlier).start()

        for h in range(c * step, (c + 1) * step):
            hc = slice(h * HEAD_DIM, (h + 1) * HEAD_DIM)
            after = sin[h]
            for b in range(sub):
                r = slice(b * block, (b + 1) * block)
                suffix = (after + gcum[h, b]).astype(BF16)
                xout[2, r, hc] = (part[0, r, hc] + dot(xin[1, r, hc], suffix, NT)).astype(BF16)
                xout[3, r, hc] = (part[1, r, hc] + dot(xin[0, r, hc], suffix, NN)).astype(BF16)
        give(1, c)

    for phase in range(2):
        for c in range(chunks):
            sent = xin.at[pl.ds(2 * phase, 2), pl.ds(0, (peers - 1) * rows), pl.ds(c * span, span)]
            pltpu.make_async_copy(sent, sent, in_send.at[phase, c]).wait()
            pltpu.make_async_copy(sent, sent, out_send.at[phase, c]).wait()
            whole = xout.at[pl.ds(2 * phase, 2), :, pl.ds(c * span, span)]
            pltpu.make_async_copy(whole, whole, out_recv.at[phase, c]).wait()
    for c in range(chunks):
        @pl.when(group < n_groups - 1)
        def _(c=c):
            state_copy(psend, pin, p_send, p_recv, c, later).wait_send()

        @pl.when(group > 0)
        def _(c=c):
            state_copy(ssend, sin, s_send, s_recv, c, earlier).wait_send()


def land(parts, *refs):
    sources, targets, sem = refs[:4], refs[4:8], refs[8]
    copies = []
    rows = sources[0].shape[0] // parts
    for part in range(parts):
        for src, dst in zip(sources, targets):
            piece = pl.ds(part * rows, rows)
            copies.append(pltpu.make_async_copy(src.at[piece], dst.at[piece], sem))
            copies[-1].start()
    for copy in copies:
        copy.wait()


def per_device(mesh, query, key, value, cotangent, gain, incoming_state):
    n_seq, n_head = mesh.shape["seq"], mesh.shape["head"]
    rows, features = query.shape
    local_heads = incoming_state.shape[0]
    sub = 1
    while sub < 4 and n_seq % (2 * sub) == 0 and local_heads % (2 * sub) == 0:
        sub *= 2
    heads = local_heads // sub
    step = max(1, heads // 4)
    chunks = heads // step
    tokens = rows * n_head * sub
    width = heads * HEAD_DIM
    plan = (n_seq // sub, sub, n_head, rows, heads, step)
    anywhere = pl.BlockSpec(memory_space=pl.ANY)
    resident = pl.BlockSpec(memory_space=pltpu.HBM)
    state = pltpu.VMEM((heads, HEAD_DIM, HEAD_DIM), F32)
    states = pltpu.VMEM((heads, sub, HEAD_DIM, HEAD_DIM), F32)
    sems = pltpu.SemaphoreType.DMA((2, chunks))
    chain = pltpu.SemaphoreType.DMA((chunks,))
    shapes = [jax.ShapeDtypeStruct((rows, features), BF16)] * 4
    results = pl.pallas_call(
        functools.partial(kernel, plan),
        out_shape=shapes,
        in_specs=[resident] * 6,
        out_specs=[anywhere] * 4,
        scratch_shapes=[
            pltpu.VMEM((4, tokens, width), BF16),
            pltpu.VMEM((4, tokens, width), BF16),
            pltpu.VMEM((2, tokens, width), F32),
            states, states, state, state, state, state, state,
            pltpu.VMEM((local_heads, HEAD_DIM), F32),
            sems, sems, sems, sems, chain, chain, chain, chain,
            pltpu.SemaphoreType.DMA,
        ],
        compiler_params=pltpu.CompilerParams(
            collective_id=0, has_side_effects=True, vmem_limit_bytes=51000 * 1024),
    )(query, key, value, cotangent, gain.reshape(local_heads, HEAD_DIM), incoming_state)
    return pl.pallas_call(
        functools.partial(land, 4 if rows % 64 == 0 else 1),
        out_shape=shapes,
        in_specs=[anywhere] * 4,
        out_specs=[anywhere] * 4,
        scratch_shapes=[pltpu.SemaphoreType.DMA],
        compiler_params=pltpu.CompilerParams(vmem_limit_bytes=1024 * 1024),
    )(*results)


def solution(mesh):
    tokens = P(("seq", "head"), None)
    return jax.shard_map(
        functools.partial(per_device, mesh),
        mesh=mesh,
        in_specs=(tokens, tokens, tokens, tokens, P("head"), P("head", None, None)),
        out_specs=(tokens, tokens, tokens, tokens),
        check_vma=False,
    )
```

```python
import functools

import jax
import jax.numpy as jnp
from jax import lax
from jax.experimental import pallas as pl
from jax.experimental.pallas import tpu as pltpu
from jax.sharding import PartitionSpec as P

HEAD_DIM = 128
EPSILON = 1e-06
MESH = pl.DeviceIdType.MESH
F32 = jnp.float32
BF16 = jnp.bfloat16

NT = (((1,), (1,)), ((), ()))
TN = (((0,), (0,)), ((), ()))
NN = (((1,), (0,)), ((), ()))


def dot(a, b, dims):
    return lax.dot_general(a, b, dims, preferred_element_type=F32)


def kernel(plan, q_hbm, k_hbm, v_hbm, y_hbm, gain_hbm, s0_hbm, o_out, gq_out, gk_out, gv_out,
           xin, xout, part, cum, gcum, prefix, tot, gtot, xt, xg, pin, psend, sin, ssend, gain,
           in_send, in_recv, out_send, out_recv, p_send, p_recv, s_send, s_recv,
           t_send, t_recv, g_send, g_recv, gain_sem, ready):
    n_outer, n_inner, sub, n_head, rows, heads, step = plan
    peers = sub * n_head
    chunks = heads // step
    block = rows * n_head
    span = step * HEAD_DIM
    seq, hd = lax.axis_index("seq"), lax.axis_index("head")
    group, j = seq // sub, lax.rem(seq, sub)
    outer, inner = group // n_inner, lax.rem(group, n_inner)
    me = j * n_head + hd

    def place(p):
        to_j = lax.rem(j + p // n_head, sub)
        to_hd = lax.rem(hd + lax.rem(p, n_head), n_head)
        return to_j * n_head + to_hd, (group * sub + to_j, to_hd)

    def column(other, c):
        owner = lax.rem(other, n_head) * (sub * heads) + (other // n_head) * heads + c * step
        return pl.ds(pl.multiple_of(owner * HEAD_DIM, span), span)

    def strip(index):
        return pl.ds(pl.multiple_of(index * rows, rows), rows)

    def cols(c):
        return pl.ds(pl.multiple_of(c * span, span), span)

    def piece(c):
        return pl.ds(c * step, step)

    across = ((outer * n_inner + (n_inner - 1 - inner)) * sub + j, hd)
    later = (seq + n_inner * sub, hd)
    earlier = (seq - n_inner * sub, hd)
    first, last = outer == 0, outer == n_outer - 1
    barrier = pltpu.get_barrier_semaphore()

    def greet(p, carry):
        _, device = place(p)
        pl.semaphore_signal(barrier, inc=1, device_id=device, device_id_type=MESH)
        return carry

    lax.fori_loop(1, peers, greet, 0)
    inside = inner == 0

    if n_inner == 2:
        @pl.when(inside)
        def _():
            pl.semaphore_signal(barrier, inc=1, device_id=across, device_id_type=MESH)

    @pl.when(jnp.logical_not(last))
    def _():
        pl.semaphore_signal(barrier, inc=1, device_id=later, device_id_type=MESH)

    sources = ((k_hbm, v_hbm), (q_hbm, y_hbm))
    targets = ((o_out, gq_out), (gk_out, gv_out))

    for more_x in range(n_inner):
        for more_z in range(2):
            @pl.when(jnp.logical_and(inner == more_x, first == (more_z == 0)))
            def _(more=more_x + more_z):
                pl.semaphore_wait(barrier, peers - 1 + more)

    for phase in range(2):
        def scatter(c, carry, phase=phase):
            def one(p, carry):
                other, device = place(p)
                for a in range(2):
                    pltpu.make_async_remote_copy(
                        src_ref=sources[phase][a].at[:, column(other, c)],
                        dst_ref=xin.at[2 * phase + a, strip(me), cols(c)],
                        send_sem=in_send.at[phase, c],
                        recv_sem=in_recv.at[phase, c],
                        device_id=device,
                        device_id_type=MESH,
                    ).start()
                return carry

            lax.fori_loop(1, peers, one, 0)
            for a in range(2):
                pltpu.make_async_copy(
                    sources[phase][a].at[:, column(me, c)],
                    xin.at[2 * phase + a, strip(me), cols(c)],
                    in_recv.at[phase, c],
                ).start()
            return carry

        lax.fori_loop(0, chunks, scatter, 0)

    gains = pltpu.make_async_copy(gain_hbm, gain, gain_sem)
    gains.start()

    if n_inner == 2:
        @pl.when(jnp.logical_not(inside))
        def _():
            pl.semaphore_signal(ready.at[0], inc=1, device_id=across, device_id_type=MESH)

    @pl.when(jnp.logical_not(first))
    def _():
        pl.semaphore_signal(ready.at[1], inc=1, device_id=earlier, device_id_type=MESH)

    @pl.when(first)
    def _():
        def carried_in(c, carry):
            pltpu.make_async_copy(
                s0_hbm.at[pl.ds(j * heads + c * step, step)], pin.at[piece(c)], p_recv.at[c],
            ).start()
            return carry

        lax.fori_loop(0, chunks, carried_in, 0)

    @pl.when(last)
    def _():
        sin[...] = jnp.zeros_like(sin)

    row = lax.broadcasted_iota(jnp.int32, (block, block), 0)
    col = lax.broadcasted_iota(jnp.int32, (block, block), 1)
    causal = col <= row
    gains.wait()

    if n_inner == 2:
        @pl.when(inside)
        def _():
            pl.semaphore_wait(ready.at[0], 1)

    @pl.when(jnp.logical_not(last))
    def _():
        pl.semaphore_wait(ready.at[1], 1)

    def arrived(phase, c):
        ref = xin.at[pl.ds(2 * phase, 2), :, cols(c)]
        pltpu.make_async_copy(ref, ref, in_recv.at[phase, c]).wait()

    def give(phase, c):
        def back(p, carry):
            other, device = place(p)
            for a in range(2):
                pltpu.make_async_remote_copy(
                    src_ref=xout.at[2 * phase + a, strip(other), cols(c)],
                    dst_ref=targets[phase][a].at[:, column(me, c)],
                    send_sem=out_send.at[phase, c],
                    recv_sem=out_recv.at[phase, c],
                    device_id=device,
                    device_id_type=MESH,
                ).start()
            return carry

        lax.fori_loop(1, peers, back, 0)
        for a in range(2):
            pltpu.make_async_copy(
                xout.at[2 * phase + a, strip(me), cols(c)],
                targets[phase][a].at[:, column(me, c)],
                out_recv.at[phase, c],
            ).start()

    def state_copy(src, dst, send, recv, c, device):
        return pltpu.make_async_remote_copy(
            src_ref=src.at[piece(c)], dst_ref=dst.at[piece(c)], send_sem=send.at[c],
            recv_sem=recv.at[c], device_id=device, device_id_type=MESH)

    def landed(ref, recv, c):
        pltpu.make_async_copy(ref.at[piece(c)], ref.at[piece(c)], recv.at[c]).wait()

    def lanes(c, h):
        return pl.ds(pl.multiple_of(c * span + h * HEAD_DIM, HEAD_DIM), HEAD_DIM)

    def block_states(c):
        arrived(0, c)
        for h in range(step):
            n, hc = c * step + h, lanes(c, h)
            run = dot(xin[0, :block, hc], xin[1, :block, hc], TN)
            for b in range(1, sub):
                r = slice(b * block, (b + 1) * block)
                cum[n, b - 1] = run
                run = run + dot(xin[0, r, hc], xin[1, r, hc], TN)
            tot[n] = run
        if n_inner == 2:
            state_copy(tot, xt, t_send, t_recv, c, across).start()

    def pass_prefix(c):
        if n_inner == 2:
            landed(xt, t_recv, c)
        landed(pin, p_recv, c)

        @pl.when(jnp.logical_not(last))
        def _():
            for h in range(step):
                n = c * step + h
                psend[n] = pin[n] + tot[n] + xt[n] if n_inner == 2 else pin[n] + tot[n]
            state_copy(psend, pin, p_send, p_recv, c, later).start()

        for h in range(step):
            n = c * step + h
            before = pin[n]
            if n_inner == 2:
                before = before + jnp.where(inner == 1, xt[n], 0.0)
            prefix[n, 0] = before.astype(BF16)
            for b in range(1, sub):
                prefix[n, b] = (before + cum[n, b - 1]).astype(BF16)

    def attend(c):
        arrived(1, c)
        for h in range(step):
            n, hc = c * step + h, lanes(c, h)
            at = pl.multiple_of((j * heads + n) * HEAD_DIM, HEAD_DIM)
            g = gain[pl.ds(at, HEAD_DIM)].reshape(1, HEAD_DIM)
            run = None
            for b in reversed(range(sub)):
                r = slice(b * block, (b + 1) * block)
                k, v, q, up = xin[0, r, hc], xin[1, r, hc], xin[2, r, hc], xin[3, r, hc]
                state = prefix[n, b]
                w = jnp.where(causal, dot(q, k, NT), 0.0).astype(BF16)
                att = dot(w, v, NN) + dot(q, state, NN)
                inv = lax.rsqrt(jnp.mean(att * att, axis=-1, keepdims=True) + EPSILON)
                normed = att * inv
                xout[0, r, hc] = (normed * g).astype(BF16)
                scaled = up.astype(F32) * g
                ga = ((scaled - normed * jnp.mean(scaled * normed, axis=-1, keepdims=True))
                      * inv).astype(BF16)
                gw = jnp.where(causal, dot(ga, v, NT), 0.0).astype(BF16)
                xout[1, r, hc] = (dot(gw, k, NN) + dot(ga, state, NT)).astype(BF16)
                part[0, r, hc] = dot(gw, q, TN)
                part[1, r, hc] = dot(w, ga, TN)
                if run is not None:
                    gcum[n, b] = run
                grad = dot(q, ga, TN)
                run = grad if run is None else run + grad
            gtot[n] = run
        if n_inner == 2:
            state_copy(gtot, xg, g_send, g_recv, c, across).start()
        give(0, c)

    def finish(c):
        if n_inner == 2:
            landed(xg, g_recv, c)

        @pl.when(jnp.logical_not(last))
        def _():
            landed(sin, s_recv, c)

        @pl.when(jnp.logical_not(first))
        def _():
            for h in range(step):
                n = c * step + h
                ssend[n] = sin[n] + gtot[n] + xg[n] if n_inner == 2 else sin[n] + gtot[n]
            state_copy(ssend, sin, s_send, s_recv, c, earlier).start()

        for h in range(step):
            n, hc = c * step + h, lanes(c, h)
            after = sin[n]
            if n_inner == 2:
                after = after + jnp.where(inner == 0, xg[n], 0.0)
            for b in range(sub):
                r = slice(b * block, (b + 1) * block)
                suffix = (after + gcum[n, b] if b < sub - 1 else after).astype(BF16)
                xout[2, r, hc] = (part[0, r, hc] + dot(xin[1, r, hc], suffix, NT)).astype(BF16)
                xout[3, r, hc] = (part[1, r, hc] + dot(xin[0, r, hc], suffix, NN)).astype(BF16)
        give(1, c)

    prefix_lag = jnp.minimum(2 + 2 * outer, chunks)
    suffix_lag = chunks + 2 + 2 * (n_outer - 1 - outer)

    def tick(i, carry):
        @pl.when(i < chunks)
        def _():
            block_states(i)

        @pl.when(jnp.logical_and(i >= prefix_lag, i < prefix_lag + chunks))
        def _():
            pass_prefix(i - prefix_lag)

        @pl.when(jnp.logical_and(i >= chunks, i < 2 * chunks))
        def _():
            attend(i - chunks)

        @pl.when(jnp.logical_and(i >= suffix_lag, i < suffix_lag + chunks))
        def _():
            finish(i - suffix_lag)

        return carry

    lax.fori_loop(0, 2 * chunks + 2 * n_outer, tick, 0)

    def drain(c, carry):
        for phase in range(2):
            sent = xin.at[pl.ds(2 * phase, 2), pl.ds(0, (peers - 1) * rows), cols(c)]
            pltpu.make_async_copy(sent, sent, in_send.at[phase, c]).wait()
            pltpu.make_async_copy(sent, sent, out_send.at[phase, c]).wait()
            whole = xout.at[pl.ds(2 * phase, 2), :, cols(c)]
            pltpu.make_async_copy(whole, whole, out_recv.at[phase, c]).wait()
        if n_inner == 2:
            state_copy(tot, xt, t_send, t_recv, c, across).wait_send()
            state_copy(gtot, xg, g_send, g_recv, c, across).wait_send()

        @pl.when(jnp.logical_not(last))
        def _():
            state_copy(psend, pin, p_send, p_recv, c, later).wait_send()

        @pl.when(jnp.logical_not(first))
        def _():
            state_copy(ssend, sin, s_send, s_recv, c, earlier).wait_send()

        return carry

    lax.fori_loop(0, chunks, drain, 0)


def land(parts, *refs):
    sources, targets, sem = refs[:4], refs[4:8], refs[8]
    copies = []
    rows = sources[0].shape[0] // parts
    for part in range(parts):
        for src, dst in zip(sources, targets):
            piece = pl.ds(part * rows, rows)
            copies.append(pltpu.make_async_copy(src.at[piece], dst.at[piece], sem))
            copies[-1].start()
    for copy in copies:
        copy.wait()


def per_device(mesh, query, key, value, cotangent, gain, incoming_state):
    n_seq, n_head = mesh.shape["seq"], mesh.shape["head"]
    rows, features = query.shape
    local_heads = incoming_state.shape[0]
    sub = 2 if n_seq % 2 == 0 and local_heads % 2 == 0 else 1
    n_inner = 2 if n_seq % (2 * sub) == 0 else 1
    n_outer = n_seq // (sub * n_inner)
    heads = local_heads // sub
    step = next(s for s in range(max(1, heads // 8), heads + 1) if heads % s == 0)
    chunks = heads // step
    tokens = rows * n_head * sub
    width = heads * HEAD_DIM
    plan = (n_outer, n_inner, sub, n_head, rows, heads, step)
    anywhere = pl.BlockSpec(memory_space=pl.ANY)
    resident = pl.BlockSpec(memory_space=pltpu.HBM)
    state = pltpu.VMEM((heads, HEAD_DIM, HEAD_DIM), F32)
    states = pltpu.VMEM((heads, max(1, sub - 1), HEAD_DIM, HEAD_DIM), F32)
    sems = pltpu.SemaphoreType.DMA((2, chunks))
    chain = pltpu.SemaphoreType.DMA((chunks,))
    shapes = [jax.ShapeDtypeStruct((rows, features), BF16)] * 4
    results = pl.pallas_call(
        functools.partial(kernel, plan),
        out_shape=shapes,
        in_specs=[resident] * 6,
        out_specs=[anywhere] * 4,
        scratch_shapes=[
            pltpu.VMEM((4, tokens, width), BF16),
            pltpu.VMEM((4, tokens, width), BF16),
            pltpu.VMEM((2, tokens, width), F32),
            states, states,
            pltpu.VMEM((heads, sub, HEAD_DIM, HEAD_DIM), BF16),
            state, state, state, state, state, state, state, state,
            pltpu.VMEM((local_heads * HEAD_DIM,), F32),
            sems, sems, sems, sems, chain, chain, chain, chain, chain, chain, chain, chain,
            pltpu.SemaphoreType.DMA, pltpu.SemaphoreType.REGULAR((2,)),
        ],
        compiler_params=pltpu.CompilerParams(
            collective_id=0, has_side_effects=True, vmem_limit_bytes=51000 * 1024),
    )(query, key, value, cotangent, pltpu.with_memory_space_constraint(gain, pltpu.HBM),
      incoming_state)
    return pl.pallas_call(
        functools.partial(land, 4 if rows % 64 == 0 else 1),
        out_shape=shapes,
        in_specs=[anywhere] * 4,
        out_specs=[anywhere] * 4,
        scratch_shapes=[pltpu.SemaphoreType.DMA],
        compiler_params=pltpu.CompilerParams(vmem_limit_bytes=1024 * 1024),
    )(*results)


def solution(mesh):
    tokens = P(("seq", "head"), None)
    return jax.shard_map(
        functools.partial(per_device, mesh),
        mesh=mesh,
        in_specs=(tokens, tokens, tokens, tokens, P("head"), P("head", None, None)),
        out_specs=(tokens, tokens, tokens, tokens),
        check_vma=False,
    )
```

```python
import functools

import jax
import jax.numpy as jnp
from jax import lax
from jax.experimental import pallas as pl
from jax.experimental.pallas import tpu as pltpu
from jax.sharding import PartitionSpec as P

HEAD_DIM = 128
EPSILON = 1e-06
MESH = pl.DeviceIdType.MESH
F32 = jnp.float32
BF16 = jnp.bfloat16

NT = (((1,), (1,)), ((), ()))
TN = (((0,), (0,)), ((), ()))
NN = (((1,), (0,)), ((), ()))


def dot(a, b, dims):
    return lax.dot_general(a, b, dims, preferred_element_type=F32)


def kernel(plan, q_hbm, k_hbm, v_hbm, y_hbm, gain_hbm, s0_hbm, o_out, gq_out, gk_out, gv_out,
           xin, xout, part, cum, gcum, prefix, tot, gtot, xt, xg, pin, psend, sin, ssend, gain,
           in_recv, chain_recv, t_recv, g_recv, in_send, out_send, out_recv,
           p_send, s_send, t_send, g_send, gain_sem, ready):
    n_outer, n_inner, sub, n_head, rows, heads, step = plan
    peers = sub * n_head
    chunks = heads // step
    block = rows * n_head
    span = step * HEAD_DIM
    seq, hd = lax.axis_index("seq"), lax.axis_index("head")
    group, j = seq // sub, lax.rem(seq, sub)
    outer, inner = group // n_inner, lax.rem(group, n_inner)
    me = j * n_head + hd

    def place(p):
        to_j = lax.rem(j + p // n_head, sub)
        to_hd = lax.rem(hd + lax.rem(p, n_head), n_head)
        return to_j * n_head + to_hd, (group * sub + to_j, to_hd)

    def column(other, c):
        owner = lax.rem(other, n_head) * (sub * heads) + (other // n_head) * heads + c * step
        return pl.ds(pl.multiple_of(owner * HEAD_DIM, span), span)

    def strip(index):
        return pl.ds(pl.multiple_of(index * rows, rows), rows)

    def cols(c):
        return pl.ds(pl.multiple_of(c * span, span), span)

    def piece(c):
        return pl.ds(c * step, step)

    across = ((outer * n_inner + (n_inner - 1 - inner)) * sub + j, hd)
    later = (seq + n_inner * sub, hd)
    earlier = (seq - n_inner * sub, hd)
    first, last = outer == 0, outer == n_outer - 1
    barrier = pltpu.get_barrier_semaphore()

    def greet(p, carry):
        _, device = place(p)
        pl.semaphore_signal(barrier, inc=1, device_id=device, device_id_type=MESH)
        return carry

    lax.fori_loop(1, peers, greet, 0)
    inside = inner == 0

    if n_inner == 2:
        @pl.when(inside)
        def _():
            pl.semaphore_signal(barrier, inc=1, device_id=across, device_id_type=MESH)

    @pl.when(jnp.logical_not(last))
    def _():
        pl.semaphore_signal(barrier, inc=1, device_id=later, device_id_type=MESH)

    sources = ((k_hbm, v_hbm), (q_hbm, y_hbm))
    targets = ((o_out, gq_out), (gk_out, gv_out))

    for more_x in range(n_inner):
        for more_z in range(2):
            @pl.when(jnp.logical_and(inner == more_x, first == (more_z == 0)))
            def _(more=more_x + more_z):
                pl.semaphore_wait(barrier, peers - 1 + more)

    for phase in range(2):
        def scatter(c, carry, phase=phase):
            def one(p, carry):
                other, device = place(p)
                for a in range(2):
                    pltpu.make_async_remote_copy(
                        src_ref=sources[phase][a].at[:, column(other, c)],
                        dst_ref=xin.at[2 * phase + a, strip(me), cols(c)],
                        send_sem=in_send,
                        recv_sem=in_recv.at[phase, c],
                        device_id=device,
                        device_id_type=MESH,
                    ).start()
                return carry

            lax.fori_loop(1, peers, one, 0)
            for a in range(2):
                pltpu.make_async_copy(
                    sources[phase][a].at[:, column(me, c)],
                    xin.at[2 * phase + a, strip(me), cols(c)],
                    in_recv.at[phase, c],
                ).start()
            return carry

        lax.fori_loop(0, chunks, scatter, 0)

    gains = pltpu.make_async_copy(gain_hbm, gain, gain_sem)
    gains.start()

    if n_inner == 2:
        @pl.when(jnp.logical_not(inside))
        def _():
            pl.semaphore_signal(ready.at[0], inc=1, device_id=across, device_id_type=MESH)

    @pl.when(jnp.logical_not(first))
    def _():
        pl.semaphore_signal(ready.at[1], inc=1, device_id=earlier, device_id_type=MESH)

    @pl.when(first)
    def _():
        def carried_in(c, carry):
            pltpu.make_async_copy(
                s0_hbm.at[pl.ds(j * heads + c * step, step)], pin.at[piece(c)], chain_recv.at[c],
            ).start()
            return carry

        lax.fori_loop(0, chunks, carried_in, 0)

    @pl.when(last)
    def _():
        sin[...] = jnp.zeros_like(sin)

    row = lax.broadcasted_iota(jnp.int32, (block, block), 0)
    col = lax.broadcasted_iota(jnp.int32, (block, block), 1)
    causal = col <= row
    gains.wait()

    if n_inner == 2:
        @pl.when(inside)
        def _():
            pl.semaphore_wait(ready.at[0], 1)

    @pl.when(jnp.logical_not(last))
    def _():
        pl.semaphore_wait(ready.at[1], 1)

    def arrived(phase, c):
        ref = xin.at[pl.ds(2 * phase, 2), :, cols(c)]
        pltpu.make_async_copy(ref, ref, in_recv.at[phase, c]).wait()

    def give(phase, c):
        def back(p, carry):
            other, device = place(p)
            for a in range(2):
                pltpu.make_async_remote_copy(
                    src_ref=xout.at[2 * phase + a, strip(other), cols(c)],
                    dst_ref=targets[phase][a].at[:, column(me, c)],
                    send_sem=out_send,
                    recv_sem=out_recv,
                    device_id=device,
                    device_id_type=MESH,
                ).start()
            return carry

        lax.fori_loop(1, peers, back, 0)
        for a in range(2):
            pltpu.make_async_copy(
                xout.at[2 * phase + a, strip(me), cols(c)],
                targets[phase][a].at[:, column(me, c)],
                out_recv,
            ).start()

    def state_copy(src, dst, send, recv, c, device):
        return pltpu.make_async_remote_copy(
            src_ref=src.at[piece(c)], dst_ref=dst.at[piece(c)], send_sem=send,
            recv_sem=recv.at[c], device_id=device, device_id_type=MESH)

    def landed(ref, recv, c):
        pltpu.make_async_copy(ref.at[piece(c)], ref.at[piece(c)], recv.at[c]).wait()

    def lanes(c, h):
        return pl.ds(pl.multiple_of(c * span + h * HEAD_DIM, HEAD_DIM), HEAD_DIM)

    def block_states(c):
        arrived(0, c)
        for h in range(step):
            n, hc = c * step + h, lanes(c, h)
            run = dot(xin[0, :block, hc], xin[1, :block, hc], TN)
            for b in range(1, sub):
                r = slice(b * block, (b + 1) * block)
                cum[n, b - 1] = run
                run = run + dot(xin[0, r, hc], xin[1, r, hc], TN)
            tot[n] = run
        if n_inner == 2:
            state_copy(tot, xt, t_send, t_recv, c, across).start()

    def pass_prefix(c):
        if n_inner == 2:
            landed(xt, t_recv, c)
        landed(pin, chain_recv, c)

        @pl.when(jnp.logical_not(last))
        def _():
            for h in range(step):
                n = c * step + h
                psend[n] = pin[n] + tot[n] + xt[n] if n_inner == 2 else pin[n] + tot[n]
            state_copy(psend, pin, p_send, chain_recv, c, later).start()

        for h in range(step):
            n = c * step + h
            before = pin[n]
            if n_inner == 2:
                before = before + jnp.where(inner == 1, xt[n], 0.0)
            prefix[n, 0] = before.astype(BF16)
            for b in range(1, sub):
                prefix[n, b] = (before + cum[n, b - 1]).astype(BF16)

    def attend(c):
        arrived(1, c)
        for h in range(step):
            n, hc = c * step + h, lanes(c, h)
            at = pl.multiple_of((j * heads + n) * HEAD_DIM, HEAD_DIM)
            g = gain[pl.ds(at, HEAD_DIM)].reshape(1, HEAD_DIM)
            run = None
            for b in reversed(range(sub)):
                r = slice(b * block, (b + 1) * block)
                k, v, q, up = xin[0, r, hc], xin[1, r, hc], xin[2, r, hc], xin[3, r, hc]
                state = prefix[n, b]
                w = jnp.where(causal, dot(q, k, NT), 0.0).astype(BF16)
                att = dot(w, v, NN) + dot(q, state, NN)
                inv = lax.rsqrt(jnp.mean(att * att, axis=-1, keepdims=True) + EPSILON)
                normed = att * inv
                xout[0, r, hc] = (normed * g).astype(BF16)
                scaled = up.astype(F32) * g
                ga = ((scaled - normed * jnp.mean(scaled * normed, axis=-1, keepdims=True))
                      * inv).astype(BF16)
                gw = jnp.where(causal, dot(ga, v, NT), 0.0).astype(BF16)
                xout[1, r, hc] = (dot(gw, k, NN) + dot(ga, state, NT)).astype(BF16)
                part[0, r, hc] = dot(gw, q, TN)
                part[1, r, hc] = dot(w, ga, TN)
                if run is not None:
                    gcum[n, b] = run
                grad = dot(q, ga, TN)
                run = grad if run is None else run + grad
            gtot[n] = run
        if n_inner == 2:
            state_copy(gtot, xg, g_send, g_recv, c, across).start()
        give(0, c)

    def finish(c):
        if n_inner == 2:
            landed(xg, g_recv, c)

        @pl.when(jnp.logical_not(last))
        def _():
            landed(sin, chain_recv, c)

        @pl.when(jnp.logical_not(first))
        def _():
            for h in range(step):
                n = c * step + h
                ssend[n] = sin[n] + gtot[n] + xg[n] if n_inner == 2 else sin[n] + gtot[n]
            state_copy(ssend, sin, s_send, chain_recv, c, earlier).start()

        for h in range(step):
            n, hc = c * step + h, lanes(c, h)
            after = sin[n]
            if n_inner == 2:
                after = after + jnp.where(inner == 0, xg[n], 0.0)
            for b in range(sub):
                r = slice(b * block, (b + 1) * block)
                suffix = (after + gcum[n, b] if b < sub - 1 else after).astype(BF16)
                xout[2, r, hc] = (part[0, r, hc] + dot(xin[1, r, hc], suffix, NT)).astype(BF16)
                xout[3, r, hc] = (part[1, r, hc] + dot(xin[0, r, hc], suffix, NN)).astype(BF16)
        give(1, c)

    prefix_lag = jnp.minimum(2 + 2 * outer, chunks)
    suffix_lag = chunks + 2 + 2 * (n_outer - 1 - outer)

    def tick(i, carry):
        @pl.when(i < chunks)
        def _():
            block_states(i)

        @pl.when(jnp.logical_and(i >= prefix_lag, i < prefix_lag + chunks))
        def _():
            pass_prefix(i - prefix_lag)

        @pl.when(jnp.logical_and(i >= chunks, i < 2 * chunks))
        def _():
            attend(i - chunks)

        @pl.when(jnp.logical_and(i >= suffix_lag, i < suffix_lag + chunks))
        def _():
            finish(i - suffix_lag)

        return carry

    lax.fori_loop(0, 2 * chunks + 2 * n_outer, tick, 0)

    sent = xin.at[:, pl.ds(0, (peers - 1) * rows)]
    pltpu.make_async_copy(sent, sent, in_send).wait()
    pltpu.make_async_copy(sent, sent, out_send).wait()
    if n_inner == 2:
        pltpu.make_async_copy(tot, tot, t_send).wait()
        pltpu.make_async_copy(gtot, gtot, g_send).wait()

    @pl.when(jnp.logical_not(last))
    def _():
        pltpu.make_async_copy(psend, psend, p_send).wait()

    @pl.when(jnp.logical_not(first))
    def _():
        pltpu.make_async_copy(ssend, ssend, s_send).wait()

    pltpu.make_async_copy(xout, xout, out_recv).wait()


def land(parts, *refs):
    sources, targets, sem = refs[:4], refs[4:8], refs[8]
    copies = []
    rows = sources[0].shape[0] // parts
    for part in range(parts):
        for src, dst in zip(sources, targets):
            piece = pl.ds(part * rows, rows)
            copies.append(pltpu.make_async_copy(src.at[piece], dst.at[piece], sem))
            copies[-1].start()
    for copy in copies:
        copy.wait()


def per_device(mesh, query, key, value, cotangent, gain, incoming_state):
    n_seq, n_head = mesh.shape["seq"], mesh.shape["head"]
    rows, features = query.shape
    local_heads = incoming_state.shape[0]
    sub = 2 if n_seq % 2 == 0 and local_heads % 2 == 0 else 1
    n_inner = 2 if n_seq % (2 * sub) == 0 else 1
    n_outer = n_seq // (sub * n_inner)
    heads = local_heads // sub
    step = next(s for s in range(max(1, heads // 8), heads + 1) if heads % s == 0)
    chunks = heads // step
    tokens = rows * n_head * sub
    width = heads * HEAD_DIM
    plan = (n_outer, n_inner, sub, n_head, rows, heads, step)
    anywhere = pl.BlockSpec(memory_space=pl.ANY)
    resident = pl.BlockSpec(memory_space=pltpu.HBM)
    state = pltpu.VMEM((heads, HEAD_DIM, HEAD_DIM), F32)
    states = pltpu.VMEM((heads, max(1, sub - 1), HEAD_DIM, HEAD_DIM), F32)
    sems = pltpu.SemaphoreType.DMA((2, chunks))
    chain = pltpu.SemaphoreType.DMA((chunks,))
    one = pltpu.SemaphoreType.DMA
    shapes = [jax.ShapeDtypeStruct((rows, features), BF16)] * 4
    results = pl.pallas_call(
        functools.partial(kernel, plan),
        out_shape=shapes,
        in_specs=[resident] * 6,
        out_specs=[anywhere] * 4,
        scratch_shapes=[
            pltpu.VMEM((4, tokens, width), BF16),
            pltpu.VMEM((4, tokens, width), BF16),
            pltpu.VMEM((2, tokens, width), F32),
            states, states,
            pltpu.VMEM((heads, sub, HEAD_DIM, HEAD_DIM), BF16),
            state, state, state, state, state, state, state, state,
            pltpu.VMEM((local_heads * HEAD_DIM,), F32),
            sems, chain, chain, chain, one, one, one, one, one, one, one, one,
            pltpu.SemaphoreType.REGULAR((2,)),
        ],
        compiler_params=pltpu.CompilerParams(
            collective_id=0, has_side_effects=True, vmem_limit_bytes=51000 * 1024),
    )(query, key, value, cotangent, pltpu.with_memory_space_constraint(gain, pltpu.HBM),
      incoming_state)
    return pl.pallas_call(
        functools.partial(land, 4 if rows % 64 == 0 else 1),
        out_shape=shapes,
        in_specs=[anywhere] * 4,
        out_specs=[anywhere] * 4,
        scratch_shapes=[pltpu.SemaphoreType.DMA],
        compiler_params=pltpu.CompilerParams(vmem_limit_bytes=1024 * 1024),
    )(*results)


def solution(mesh):
    tokens = P(("seq", "head"), None)
    return jax.shard_map(
        functools.partial(per_device, mesh),
        mesh=mesh,
        in_specs=(tokens, tokens, tokens, tokens, P("head"), P("head", None, None)),
        out_specs=(tokens, tokens, tokens, tokens),
        check_vma=False,
    )
```

```python
import functools

import jax
import jax.numpy as jnp
from jax import lax
from jax.experimental import pallas as pl
from jax.experimental.pallas import tpu as pltpu
from jax.sharding import PartitionSpec as P

HEAD_DIM = 128
EPSILON = 1e-06
DETOUR_ARRAYS, DETOUR_CHUNKS = 1, 1
MESH = pl.DeviceIdType.MESH
F32 = jnp.float32
BF16 = jnp.bfloat16

NT = (((1,), (1,)), ((), ()))
TN = (((0,), (0,)), ((), ()))
NN = (((1,), (0,)), ((), ()))


def dot(a, b, dims):
    return lax.dot_general(a, b, dims, preferred_element_type=F32)


def kernel(plan, q_hbm, k_hbm, v_hbm, y_hbm, gain_hbm, s0_hbm, o_out, gq_out, gk_out, gv_out,
           xin, xout, part, cum, gcum, prefix, tot, gtot, xt, xg, pin, psend, sin, ssend, gain, hop,
           in_recv, chain_recv, t_recv, g_recv, in_send, out_send, out_recv,
           p_send, s_send, t_send, g_send, gain_sem, hop_send, hop_recv, ready):
    n_outer, n_inner, sub, n_head, rows, heads, step = plan
    peers = sub * n_head
    chunks = heads // step
    block = rows * n_head
    span = step * HEAD_DIM
    seq, hd = lax.axis_index("seq"), lax.axis_index("head")
    group, j = seq // sub, lax.rem(seq, sub)
    outer, inner = group // n_inner, lax.rem(group, n_inner)
    me = j * n_head + hd

    def place(p):
        to_j = lax.rem(j + p // n_head, sub)
        to_hd = lax.rem(hd + lax.rem(p, n_head), n_head)
        return to_j * n_head + to_hd, (group * sub + to_j, to_hd)

    def column(other, c):
        owner = lax.rem(other, n_head) * (sub * heads) + (other // n_head) * heads + c * step
        return pl.ds(pl.multiple_of(owner * HEAD_DIM, span), span)

    def strip(index):
        return pl.ds(pl.multiple_of(index * rows, rows), rows)

    def cols(c):
        return pl.ds(pl.multiple_of(c * span, span), span)

    def piece(c):
        return pl.ds(c * step, step)

    across = ((outer * n_inner + (n_inner - 1 - inner)) * sub + j, hd)
    later = (seq + n_inner * sub, hd)
    earlier = (seq - n_inner * sub, hd)
    first, last = outer == 0, outer == n_outer - 1
    detours = n_inner == 2 and n_head == 2
    partner = (seq, n_head - 1 - hd)
    hop_device = (across[0], n_head - 1 - hd)
    owes = jnp.logical_and(group == 0, hd == 1)
    owed = jnp.logical_and(group == 0, hd == 0)
    relays = jnp.logical_and(group == 1, hd == 0)
    barrier = pltpu.get_barrier_semaphore()

    def greet(p, carry):
        _, device = place(p)
        pl.semaphore_signal(barrier, inc=1, device_id=device, device_id_type=MESH)
        return carry

    lax.fori_loop(1, peers, greet, 0)
    inside = inner == 0

    if n_inner == 2:
        @pl.when(inside)
        def _():
            pl.semaphore_signal(barrier, inc=1, device_id=across, device_id_type=MESH)

    @pl.when(jnp.logical_not(last))
    def _():
        pl.semaphore_signal(barrier, inc=1, device_id=later, device_id_type=MESH)

    sources = ((k_hbm, v_hbm), (q_hbm, y_hbm))
    targets = ((o_out, gq_out), (gk_out, gv_out))

    for more_x in range(n_inner):
        for more_z in range(2):
            @pl.when(jnp.logical_and(inner == more_x, first == (more_z == 0)))
            def _(more=more_x + more_z):
                pl.semaphore_wait(barrier, peers - 1 + more)

    for phase in range(2):
        def scatter(c, carry, phase=phase):
            def one(p, carry):
                other, device = place(p)
                for a in range(2):
                    pltpu.make_async_remote_copy(
                        src_ref=sources[phase][a].at[:, column(other, c)],
                        dst_ref=xin.at[2 * phase + a, strip(me), cols(c)],
                        send_sem=in_send,
                        recv_sem=in_recv.at[phase, c],
                        device_id=device,
                        device_id_type=MESH,
                    ).start()
                return carry

            lax.fori_loop(1, peers, one, 0)
            for a in range(2):
                pltpu.make_async_copy(
                    sources[phase][a].at[:, column(me, c)],
                    xin.at[2 * phase + a, strip(me), cols(c)],
                    in_recv.at[phase, c],
                ).start()
            return carry

        lax.fori_loop(0, chunks, scatter, 0)

    gains = pltpu.make_async_copy(gain_hbm, gain, gain_sem)
    gains.start()

    if n_inner == 2:
        @pl.when(jnp.logical_not(inside))
        def _():
            pl.semaphore_signal(ready.at[0], inc=1, device_id=across, device_id_type=MESH)

    @pl.when(jnp.logical_not(first))
    def _():
        pl.semaphore_signal(ready.at[1], inc=1, device_id=earlier, device_id_type=MESH)

    @pl.when(first)
    def _():
        def carried_in(c, carry):
            pltpu.make_async_copy(
                s0_hbm.at[pl.ds(j * heads + c * step, step)], pin.at[piece(c)], chain_recv.at[c],
            ).start()
            return carry

        lax.fori_loop(0, chunks, carried_in, 0)

    @pl.when(last)
    def _():
        sin[...] = jnp.zeros_like(sin)

    row = lax.broadcasted_iota(jnp.int32, (block, block), 0)
    col = lax.broadcasted_iota(jnp.int32, (block, block), 1)
    causal = col <= row
    gains.wait()

    if n_inner == 2:
        @pl.when(inside)
        def _():
            pl.semaphore_wait(ready.at[0], 1)

    if detours:
        @pl.when(owed)
        def _():
            pl.semaphore_signal(ready.at[2], inc=1, device_id=partner, device_id_type=MESH)

        @pl.when(owes)
        def _():
            pl.semaphore_wait(ready.at[2], 1)

    @pl.when(jnp.logical_not(last))
    def _():
        pl.semaphore_wait(ready.at[1], 1)

    def arrived(phase, c):
        ref = xin.at[pl.ds(2 * phase, 2), :, cols(c)]
        pltpu.make_async_copy(ref, ref, in_recv.at[phase, c]).wait()

    def give(phase, c):
        def back(p, carry):
            other, device = place(jnp.where(group == 1, peers - p, p))
            for a in range(2):
                def send(dst, device, recv, a=a):
                    pltpu.make_async_remote_copy(
                        src_ref=xout.at[2 * phase + a, strip(other), cols(c)], dst_ref=dst,
                        send_sem=out_send, recv_sem=recv, device_id=device, device_id_type=MESH,
                    ).start()

                target = targets[phase][a].at[:, column(me, c)]
                if detours and phase == 0 and a < DETOUR_ARRAYS:
                    detour = jnp.logical_and(owes, jnp.logical_and(c < DETOUR_CHUNKS, p == 1))

                    @pl.when(detour)
                    def _():
                        send(hop.at[a, :, cols(c)], hop_device, hop_recv)

                    @pl.when(jnp.logical_not(detour))
                    def _():
                        send(target, device, out_recv)
                else:
                    send(target, device, out_recv)
            return carry

        lax.fori_loop(1, peers, back, 0)
        for a in range(2):
            pltpu.make_async_copy(
                xout.at[2 * phase + a, strip(me), cols(c)],
                targets[phase][a].at[:, column(me, c)],
                out_recv,
            ).start()

    def state_copy(src, dst, send, recv, c, device):
        return pltpu.make_async_remote_copy(
            src_ref=src.at[piece(c)], dst_ref=dst.at[piece(c)], send_sem=send,
            recv_sem=recv.at[c], device_id=device, device_id_type=MESH)

    def landed(ref, recv, c):
        pltpu.make_async_copy(ref.at[piece(c)], ref.at[piece(c)], recv.at[c]).wait()

    def lanes(c, h):
        return pl.ds(pl.multiple_of(c * span + h * HEAD_DIM, HEAD_DIM), HEAD_DIM)

    def block_states(c):
        arrived(0, c)
        for h in range(step):
            n, hc = c * step + h, lanes(c, h)
            run = dot(xin[0, :block, hc], xin[1, :block, hc], TN)
            for b in range(1, sub):
                r = slice(b * block, (b + 1) * block)
                cum[n, b - 1] = run
                run = run + dot(xin[0, r, hc], xin[1, r, hc], TN)
            tot[n] = run
        if n_inner == 2:
            state_copy(tot, xt, t_send, t_recv, c, across).start()

    def pass_prefix(c):
        if n_inner == 2:
            landed(xt, t_recv, c)
        landed(pin, chain_recv, c)

        @pl.when(jnp.logical_not(last))
        def _():
            for h in range(step):
                n = c * step + h
                psend[n] = pin[n] + tot[n] + xt[n] if n_inner == 2 else pin[n] + tot[n]
            state_copy(psend, pin, p_send, chain_recv, c, later).start()

        for h in range(step):
            n = c * step + h
            before = pin[n]
            if n_inner == 2:
                before = before + jnp.where(inner == 1, xt[n], 0.0)
            prefix[n, 0] = before.astype(BF16)
            for b in range(1, sub):
                prefix[n, b] = (before + cum[n, b - 1]).astype(BF16)

    def attend(c):
        arrived(1, c)
        for h in range(step):
            n, hc = c * step + h, lanes(c, h)
            at = pl.multiple_of((j * heads + n) * HEAD_DIM, HEAD_DIM)
            g = gain[pl.ds(at, HEAD_DIM)].reshape(1, HEAD_DIM)
            run = None
            for b in reversed(range(sub)):
                r = slice(b * block, (b + 1) * block)
                k, v, q, up = xin[0, r, hc], xin[1, r, hc], xin[2, r, hc], xin[3, r, hc]
                state = prefix[n, b]
                w = jnp.where(causal, dot(q, k, NT), 0.0).astype(BF16)
                att = dot(w, v, NN) + dot(q, state, NN)
                inv = lax.rsqrt(jnp.mean(att * att, axis=-1, keepdims=True) + EPSILON)
                normed = att * inv
                xout[0, r, hc] = (normed * g).astype(BF16)
                scaled = up.astype(F32) * g
                ga = ((scaled - normed * jnp.mean(scaled * normed, axis=-1, keepdims=True))
                      * inv).astype(BF16)
                gw = jnp.where(causal, dot(ga, v, NT), 0.0).astype(BF16)
                xout[1, r, hc] = (dot(gw, k, NN) + dot(ga, state, NT)).astype(BF16)
                part[0, r, hc] = dot(gw, q, TN)
                part[1, r, hc] = dot(w, ga, TN)
                if run is not None:
                    gcum[n, b] = run
                grad = dot(q, ga, TN)
                run = grad if run is None else run + grad
            gtot[n] = run
        if n_inner == 2:
            state_copy(gtot, xg, g_send, g_recv, c, across).start()
        give(0, c)

    def finish(c):
        if n_inner == 2:
            landed(xg, g_recv, c)

        @pl.when(jnp.logical_not(last))
        def _():
            landed(sin, chain_recv, c)

        @pl.when(jnp.logical_not(first))
        def _():
            for h in range(step):
                n = c * step + h
                ssend[n] = sin[n] + gtot[n] + xg[n] if n_inner == 2 else sin[n] + gtot[n]
            state_copy(ssend, sin, s_send, chain_recv, c, earlier).start()

        for h in range(step):
            n, hc = c * step + h, lanes(c, h)
            after = sin[n]
            if n_inner == 2:
                after = after + jnp.where(inner == 0, xg[n], 0.0)
            for b in range(sub):
                r = slice(b * block, (b + 1) * block)
                suffix = (after + gcum[n, b] if b < sub - 1 else after).astype(BF16)
                xout[2, r, hc] = (part[0, r, hc] + dot(xin[1, r, hc], suffix, NT)).astype(BF16)
                xout[3, r, hc] = (part[1, r, hc] + dot(xin[0, r, hc], suffix, NN)).astype(BF16)
        give(1, c)

    prefix_lag = jnp.minimum(2 + 2 * outer, chunks)
    suffix_lag = chunks + 2 + 2 * (n_outer - 1 - outer)

    def tick(i, carry):
        @pl.when(i < chunks)
        def _():
            block_states(i)

        @pl.when(jnp.logical_and(i >= prefix_lag, i < prefix_lag + chunks))
        def _():
            pass_prefix(i - prefix_lag)

        @pl.when(jnp.logical_and(i >= chunks, i < 2 * chunks))
        def _():
            attend(i - chunks)

        @pl.when(jnp.logical_and(i >= suffix_lag, i < suffix_lag + chunks))
        def _():
            finish(i - suffix_lag)

        return carry

    lax.fori_loop(0, 2 * chunks + 2 * n_outer, tick, 0)

    if detours:
        @pl.when(relays)
        def _():
            pltpu.make_async_copy(hop, hop, hop_recv).wait()
            whole = pl.ds(pl.multiple_of((sub * heads + j * heads) * HEAD_DIM, span), hop.shape[2])
            for a in range(DETOUR_ARRAYS):
                pltpu.make_async_remote_copy(
                    src_ref=hop.at[a], dst_ref=targets[0][a].at[:, whole], send_sem=hop_send,
                    recv_sem=out_recv, device_id=across, device_id_type=MESH).start()
            pltpu.make_async_copy(hop, hop, hop_send).wait()

    sent = xin.at[:, pl.ds(0, (peers - 1) * rows)]
    pltpu.make_async_copy(sent, sent, in_send).wait()
    pltpu.make_async_copy(sent, sent, out_send).wait()
    if n_inner == 2:
        pltpu.make_async_copy(tot, tot, t_send).wait()
        pltpu.make_async_copy(gtot, gtot, g_send).wait()

    @pl.when(jnp.logical_not(last))
    def _():
        pltpu.make_async_copy(psend, psend, p_send).wait()

    @pl.when(jnp.logical_not(first))
    def _():
        pltpu.make_async_copy(ssend, ssend, s_send).wait()

    pltpu.make_async_copy(xout, xout, out_recv).wait()


def land(parts, *refs):
    sources, targets, sem = refs[:4], refs[4:8], refs[8]
    copies = []
    rows = sources[0].shape[0] // parts
    for part in range(parts):
        for src, dst in zip(sources, targets):
            piece = pl.ds(part * rows, rows)
            copies.append(pltpu.make_async_copy(src.at[piece], dst.at[piece], sem))
            copies[-1].start()
    for copy in copies:
        copy.wait()


def per_device(mesh, query, key, value, cotangent, gain, incoming_state):
    n_seq, n_head = mesh.shape["seq"], mesh.shape["head"]
    rows, features = query.shape
    local_heads = incoming_state.shape[0]
    sub = 2 if n_seq % 2 == 0 and local_heads % 2 == 0 else 1
    n_inner = 2 if n_seq % (2 * sub) == 0 else 1
    n_outer = n_seq // (sub * n_inner)
    heads = local_heads // sub
    step = next(s for s in range(max(1, heads // 8), heads + 1) if heads % s == 0)
    chunks = heads // step
    tokens = rows * n_head * sub
    width = heads * HEAD_DIM
    plan = (n_outer, n_inner, sub, n_head, rows, heads, step)
    anywhere = pl.BlockSpec(memory_space=pl.ANY)
    resident = pl.BlockSpec(memory_space=pltpu.HBM)
    state = pltpu.VMEM((heads, HEAD_DIM, HEAD_DIM), F32)
    states = pltpu.VMEM((heads, max(1, sub - 1), HEAD_DIM, HEAD_DIM), F32)
    sems = pltpu.SemaphoreType.DMA((2, chunks))
    chain = pltpu.SemaphoreType.DMA((chunks,))
    one = pltpu.SemaphoreType.DMA
    shapes = [jax.ShapeDtypeStruct((rows, features), BF16)] * 4
    results = pl.pallas_call(
        functools.partial(kernel, plan),
        out_shape=shapes,
        in_specs=[resident] * 6,
        out_specs=[anywhere] * 4,
        scratch_shapes=[
            pltpu.VMEM((4, tokens, width), BF16),
            pltpu.VMEM((4, tokens, width), BF16),
            pltpu.VMEM((2, tokens, width), F32),
            states, states,
            pltpu.VMEM((heads, sub, HEAD_DIM, HEAD_DIM), BF16),
            state, state, state, state, state, state, state, state,
            pltpu.VMEM((local_heads * HEAD_DIM,), F32),
            pltpu.VMEM((DETOUR_ARRAYS, rows, DETOUR_CHUNKS * step * HEAD_DIM), BF16),
            sems, chain, chain, chain, one, one, one, one, one, one, one, one, one, one,
            pltpu.SemaphoreType.REGULAR((3,)),
        ],
        compiler_params=pltpu.CompilerParams(
            collective_id=0, has_side_effects=True, vmem_limit_bytes=51000 * 1024),
    )(query, key, value, cotangent, pltpu.with_memory_space_constraint(gain, pltpu.HBM),
      incoming_state)
    return pl.pallas_call(
        functools.partial(land, 4 if rows % 64 == 0 else 1),
        out_shape=shapes,
        in_specs=[anywhere] * 4,
        out_specs=[anywhere] * 4,
        scratch_shapes=[pltpu.SemaphoreType.DMA],
        compiler_params=pltpu.CompilerParams(vmem_limit_bytes=1024 * 1024),
    )(*results)


def solution(mesh):
    tokens = P(("seq", "head"), None)
    return jax.shard_map(
        functools.partial(per_device, mesh),
        mesh=mesh,
        in_specs=(tokens, tokens, tokens, tokens, P("head"), P("head", None, None)),
        out_specs=(tokens, tokens, tokens, tokens),
        check_vma=False,
    )
```

```python
import functools

import jax
import jax.numpy as jnp
from jax import lax
from jax.experimental import pallas as pl
from jax.experimental.pallas import tpu as pltpu
from jax.sharding import PartitionSpec as P

HEAD_DIM = 128
EPSILON = 1e-06
DETOUR_ARRAYS, DETOUR_CHUNKS = 1, 1
MESH = pl.DeviceIdType.MESH
F32 = jnp.float32
BF16 = jnp.bfloat16

NT = (((1,), (1,)), ((), ()))
TN = (((0,), (0,)), ((), ()))
NN = (((1,), (0,)), ((), ()))


def dot(a, b, dims):
    return lax.dot_general(a, b, dims, preferred_element_type=F32)


def kernel(plan, q_hbm, k_hbm, v_hbm, y_hbm, gain_hbm, s0_hbm, o_out, gq_out, gk_out, gv_out,
           xin, xout, part, cum, gcum, prefix, tot, gtot, xt, xg, pin, psend, sin, ssend, gain, hop,
           first_recv, in_send, entered):
    n_outer, n_inner, sub, n_head, rows, heads, step = plan
    peers = sub * n_head
    chunks = heads // step
    block = rows * n_head
    span = step * HEAD_DIM
    seq, hd = lax.axis_index("seq"), lax.axis_index("head")
    group, j = seq // sub, lax.rem(seq, sub)
    outer, inner = group // n_inner, lax.rem(group, n_inner)
    me = j * n_head + hd

    def place(p):
        to_j = lax.rem(j + p // n_head, sub)
        to_hd = lax.rem(hd + lax.rem(p, n_head), n_head)
        return to_j * n_head + to_hd, (group * sub + to_j, to_hd)

    def column(other, c):
        owner = lax.rem(other, n_head) * (sub * heads) + (other // n_head) * heads + c * step
        return pl.ds(pl.multiple_of(owner * HEAD_DIM, span), span)

    def strip(index):
        return pl.ds(pl.multiple_of(index * rows, rows), rows)

    def cols(c):
        return pl.ds(pl.multiple_of(c * span, span), span)

    def piece(c):
        return pl.ds(c * step, step)

    across = ((outer * n_inner + (n_inner - 1 - inner)) * sub + j, hd)
    later = (seq + n_inner * sub, hd)
    earlier = (seq - n_inner * sub, hd)
    first, last = outer == 0, outer == n_outer - 1
    detours = n_inner == 2 and n_head == 2
    partner = (seq, n_head - 1 - hd)
    hop_device = (across[0], n_head - 1 - hd)
    owes = jnp.logical_and(group == 0, hd == 1)
    owed = jnp.logical_and(group == 0, hd == 0)
    relays = jnp.logical_and(group == 1, hd == 0)
    barrier = pltpu.get_barrier_semaphore()

    def greet(p, carry):
        _, device = place(p)
        pl.semaphore_signal(barrier, inc=1, device_id=device, device_id_type=MESH)
        return carry

    lax.fori_loop(1, peers, greet, 0)
    inside = inner == 0

    if n_inner == 2:
        @pl.when(inside)
        def _():
            pl.semaphore_signal(barrier, inc=1, device_id=across, device_id_type=MESH)

    @pl.when(jnp.logical_not(last))
    def _():
        pl.semaphore_signal(barrier, inc=1, device_id=later, device_id_type=MESH)

    sources = ((k_hbm, v_hbm), (q_hbm, y_hbm))
    targets = ((o_out, gq_out), (gk_out, gv_out))

    for more_x in range(n_inner):
        for more_z in range(2):
            @pl.when(jnp.logical_and(inner == more_x, first == (more_z == 0)))
            def _(more=more_x + more_z):
                pl.semaphore_wait(barrier, peers - 1 + more)

    def scatter(phase, recv):
        def chunk(c, carry):
            def one(p, carry):
                other, device = place(p)
                for a in range(2):
                    pltpu.make_async_remote_copy(
                        src_ref=sources[phase][a].at[:, column(other, c)],
                        dst_ref=xin.at[2 * phase + a, strip(me), cols(c)],
                        send_sem=in_send,
                        recv_sem=recv.at[c],
                        device_id=device,
                        device_id_type=MESH,
                    ).start()
                return carry

            lax.fori_loop(1, peers, one, 0)
            for a in range(2):
                pltpu.make_async_copy(
                    sources[phase][a].at[:, column(me, c)],
                    xin.at[2 * phase + a, strip(me), cols(c)],
                    recv.at[c],
                ).start()
            return carry

        lax.fori_loop(0, chunks, chunk, 0)

    scatter(0, first_recv)

    def rest(second_recv, chain_recv, t_recv, g_recv, out_send, out_recv,
             p_send, s_send, t_send, g_send, gain_sem, hop_send, hop_recv):
        in_recv = first_recv, second_recv

        def announce(p, carry):
            _, device = place(p)
            pl.semaphore_signal(entered.at[0], inc=1, device_id=device, device_id_type=MESH)
            return carry

        lax.fori_loop(1, peers, announce, 0)
        gains = pltpu.make_async_copy(gain_hbm, gain, gain_sem)
        gains.start()

        if n_inner == 2:
            @pl.when(jnp.logical_not(inside))
            def _():
                pl.semaphore_signal(entered.at[0], inc=1, device_id=across, device_id_type=MESH)

        @pl.when(jnp.logical_not(first))
        def _():
            pl.semaphore_signal(entered.at[0], inc=1, device_id=earlier, device_id_type=MESH)

        @pl.when(first)
        def _():
            def carried_in(c, carry):
                pltpu.make_async_copy(
                    s0_hbm.at[pl.ds(j * heads + c * step, step)], pin.at[piece(c)], chain_recv.at[c],
                ).start()
                return carry

            lax.fori_loop(0, chunks, carried_in, 0)

        @pl.when(last)
        def _():
            sin[...] = jnp.zeros_like(sin)

        row = lax.broadcasted_iota(jnp.int32, (block, block), 0)
        col = lax.broadcasted_iota(jnp.int32, (block, block), 1)
        causal = col <= row
        gains.wait()

        for more_x in range(n_inner):
            for more_z in range(2):
                @pl.when(jnp.logical_and(inner == n_inner - 1 - more_x, last == (more_z == 0)))
                def _(more=more_x + more_z):
                    pl.semaphore_wait(entered.at[0], peers - 1 + more)

        if n_inner == 2:
            @pl.when(inside)
            def _():
                pl.semaphore_signal(entered.at[1], inc=1, device_id=across, device_id_type=MESH)

        @pl.when(jnp.logical_not(last))
        def _():
            pl.semaphore_signal(entered.at[1], inc=1, device_id=later, device_id_type=MESH)

        if detours:
            @pl.when(owed)
            def _():
                pl.semaphore_signal(entered.at[2], inc=1, device_id=partner, device_id_type=MESH)

        scatter(1, second_recv)

        for more_x in range(n_inner):
            for more_z in range(2):
                if more_x + more_z > 0:
                    @pl.when(jnp.logical_and(inner == more_x, first == (more_z == 0)))
                    def _(more=more_x + more_z):
                        pl.semaphore_wait(entered.at[1], more)

        if detours:
            @pl.when(owes)
            def _():
                pl.semaphore_wait(entered.at[2], 1)

        def arrived(phase, c):
            ref = xin.at[pl.ds(2 * phase, 2), :, cols(c)]
            pltpu.make_async_copy(ref, ref, in_recv[phase].at[c]).wait()

        def give(phase, c):
            def back(p, carry):
                other, device = place(jnp.where(group == 1, peers - p, p))
                for a in range(2):
                    def send(dst, device, recv, a=a):
                        pltpu.make_async_remote_copy(
                            src_ref=xout.at[2 * phase + a, strip(other), cols(c)], dst_ref=dst,
                            send_sem=out_send, recv_sem=recv, device_id=device, device_id_type=MESH,
                        ).start()

                    target = targets[phase][a].at[:, column(me, c)]
                    if detours and phase == 0 and a < DETOUR_ARRAYS:
                        detour = jnp.logical_and(owes, jnp.logical_and(c < DETOUR_CHUNKS, p == 1))

                        @pl.when(detour)
                        def _():
                            send(hop.at[a, :, cols(c)], hop_device, hop_recv)

                        @pl.when(jnp.logical_not(detour))
                        def _():
                            send(target, device, out_recv)
                    else:
                        send(target, device, out_recv)
                return carry

            lax.fori_loop(1, peers, back, 0)
            for a in range(2):
                pltpu.make_async_copy(
                    xout.at[2 * phase + a, strip(me), cols(c)],
                    targets[phase][a].at[:, column(me, c)],
                    out_recv,
                ).start()

        def state_copy(src, dst, send, recv, c, device):
            return pltpu.make_async_remote_copy(
                src_ref=src.at[piece(c)], dst_ref=dst.at[piece(c)], send_sem=send,
                recv_sem=recv.at[c], device_id=device, device_id_type=MESH)

        def landed(ref, recv, c):
            pltpu.make_async_copy(ref.at[piece(c)], ref.at[piece(c)], recv.at[c]).wait()

        def lanes(c, h):
            return pl.ds(pl.multiple_of(c * span + h * HEAD_DIM, HEAD_DIM), HEAD_DIM)

        def block_states(c):
            arrived(0, c)
            for h in range(step):
                n, hc = c * step + h, lanes(c, h)
                run = dot(xin[0, :block, hc], xin[1, :block, hc], TN)
                for b in range(1, sub):
                    r = slice(b * block, (b + 1) * block)
                    cum[n, b - 1] = run
                    run = run + dot(xin[0, r, hc], xin[1, r, hc], TN)
                tot[n] = run
            if n_inner == 2:
                state_copy(tot, xt, t_send, t_recv, c, across).start()

        def pass_prefix(c):
            if n_inner == 2:
                landed(xt, t_recv, c)
            landed(pin, chain_recv, c)

            @pl.when(jnp.logical_not(last))
            def _():
                for h in range(step):
                    n = c * step + h
                    psend[n] = pin[n] + tot[n] + xt[n] if n_inner == 2 else pin[n] + tot[n]
                state_copy(psend, pin, p_send, chain_recv, c, later).start()

            for h in range(step):
                n = c * step + h
                before = pin[n]
                if n_inner == 2:
                    before = before + jnp.where(inner == 1, xt[n], 0.0)
                prefix[n, 0] = before.astype(BF16)
                for b in range(1, sub):
                    prefix[n, b] = (before + cum[n, b - 1]).astype(BF16)

        def attend(c):
            arrived(1, c)
            for h in range(step):
                n, hc = c * step + h, lanes(c, h)
                at = pl.multiple_of((j * heads + n) * HEAD_DIM, HEAD_DIM)
                g = gain[pl.ds(at, HEAD_DIM)].reshape(1, HEAD_DIM)
                run = None
                for b in reversed(range(sub)):
                    r = slice(b * block, (b + 1) * block)
                    k, v, q, up = xin[0, r, hc], xin[1, r, hc], xin[2, r, hc], xin[3, r, hc]
                    state = prefix[n, b]
                    w = jnp.where(causal, dot(q, k, NT), 0.0).astype(BF16)
                    att = dot(w, v, NN) + dot(q, state, NN)
                    inv = lax.rsqrt(jnp.mean(att * att, axis=-1, keepdims=True) + EPSILON)
                    normed = att * inv
                    xout[0, r, hc] = (normed * g).astype(BF16)
                    scaled = up.astype(F32) * g
                    ga = ((scaled - normed * jnp.mean(scaled * normed, axis=-1, keepdims=True))
                          * inv).astype(BF16)
                    gw = jnp.where(causal, dot(ga, v, NT), 0.0).astype(BF16)
                    xout[1, r, hc] = (dot(gw, k, NN) + dot(ga, state, NT)).astype(BF16)
                    part[0, r, hc] = dot(gw, q, TN)
                    part[1, r, hc] = dot(w, ga, TN)
                    if run is not None:
                        gcum[n, b] = run
                    grad = dot(q, ga, TN)
                    run = grad if run is None else run + grad
                gtot[n] = run
            if n_inner == 2:
                state_copy(gtot, xg, g_send, g_recv, c, across).start()
            give(0, c)

        def finish(c):
            if n_inner == 2:
                landed(xg, g_recv, c)

            @pl.when(jnp.logical_not(last))
            def _():
                landed(sin, chain_recv, c)

            @pl.when(jnp.logical_not(first))
            def _():
                for h in range(step):
                    n = c * step + h
                    ssend[n] = sin[n] + gtot[n] + xg[n] if n_inner == 2 else sin[n] + gtot[n]
                state_copy(ssend, sin, s_send, chain_recv, c, earlier).start()

            for h in range(step):
                n, hc = c * step + h, lanes(c, h)
                after = sin[n]
                if n_inner == 2:
                    after = after + jnp.where(inner == 0, xg[n], 0.0)
                for b in range(sub):
                    r = slice(b * block, (b + 1) * block)
                    suffix = (after + gcum[n, b] if b < sub - 1 else after).astype(BF16)
                    xout[2, r, hc] = (part[0, r, hc] + dot(xin[1, r, hc], suffix, NT)).astype(BF16)
                    xout[3, r, hc] = (part[1, r, hc] + dot(xin[0, r, hc], suffix, NN)).astype(BF16)
            give(1, c)

        prefix_lag = jnp.minimum(2 + 2 * outer, chunks)
        suffix_lag = chunks + 2 + 2 * (n_outer - 1 - outer)

        def tick(i, carry):
            @pl.when(i < chunks)
            def _():
                block_states(i)

            @pl.when(jnp.logical_and(i >= prefix_lag, i < prefix_lag + chunks))
            def _():
                pass_prefix(i - prefix_lag)

            @pl.when(jnp.logical_and(i >= chunks, i < 2 * chunks))
            def _():
                attend(i - chunks)

            @pl.when(jnp.logical_and(i >= suffix_lag, i < suffix_lag + chunks))
            def _():
                finish(i - suffix_lag)

            return carry

        lax.fori_loop(0, 2 * chunks + 2 * n_outer, tick, 0)

        if detours:
            @pl.when(relays)
            def _():
                pltpu.make_async_copy(hop, hop, hop_recv).wait()
                whole = pl.ds(pl.multiple_of((sub * heads + j * heads) * HEAD_DIM, span), hop.shape[2])
                for a in range(DETOUR_ARRAYS):
                    pltpu.make_async_remote_copy(
                        src_ref=hop.at[a], dst_ref=targets[0][a].at[:, whole], send_sem=hop_send,
                        recv_sem=out_recv, device_id=across, device_id_type=MESH).start()
                pltpu.make_async_copy(hop, hop, hop_send).wait()

        sent = xin.at[:, pl.ds(0, (peers - 1) * rows)]
        pltpu.make_async_copy(sent, sent, in_send).wait()
        pltpu.make_async_copy(sent, sent, out_send).wait()
        if n_inner == 2:
            pltpu.make_async_copy(tot, tot, t_send).wait()
            pltpu.make_async_copy(gtot, gtot, g_send).wait()

        @pl.when(jnp.logical_not(last))
        def _():
            pltpu.make_async_copy(psend, psend, p_send).wait()

        @pl.when(jnp.logical_not(first))
        def _():
            pltpu.make_async_copy(ssend, ssend, s_send).wait()

        pltpu.make_async_copy(xout, xout, out_recv).wait()

    one = pltpu.SemaphoreType.DMA
    chain = one((chunks,))
    pl.run_scoped(rest, chain, chain, chain, chain, *[one] * 9)


def land(parts, *refs):
    sources, targets, sem = refs[:4], refs[4:8], refs[8]
    copies = []
    rows = sources[0].shape[0] // parts
    for part in range(parts):
        for src, dst in zip(sources, targets):
            piece = pl.ds(part * rows, rows)
            copies.append(pltpu.make_async_copy(src.at[piece], dst.at[piece], sem))
            copies[-1].start()
    for copy in copies:
        copy.wait()


def per_device(mesh, query, key, value, cotangent, gain, incoming_state):
    n_seq, n_head = mesh.shape["seq"], mesh.shape["head"]
    rows, features = query.shape
    local_heads = incoming_state.shape[0]
    sub = 2 if n_seq % 2 == 0 and local_heads % 2 == 0 else 1
    n_inner = 2 if n_seq % (2 * sub) == 0 else 1
    n_outer = n_seq // (sub * n_inner)
    heads = local_heads // sub
    step = next(s for s in range(max(1, heads // 8), heads + 1) if heads % s == 0)
    chunks = heads // step
    tokens = rows * n_head * sub
    width = heads * HEAD_DIM
    plan = (n_outer, n_inner, sub, n_head, rows, heads, step)
    anywhere = pl.BlockSpec(memory_space=pl.ANY)
    resident = pl.BlockSpec(memory_space=pltpu.HBM)
    state = pltpu.VMEM((heads, HEAD_DIM, HEAD_DIM), F32)
    states = pltpu.VMEM((heads, max(1, sub - 1), HEAD_DIM, HEAD_DIM), F32)
    shapes = [jax.ShapeDtypeStruct((rows, features), BF16)] * 4
    results = pl.pallas_call(
        functools.partial(kernel, plan),
        out_shape=shapes,
        in_specs=[resident] * 6,
        out_specs=[anywhere] * 4,
        scratch_shapes=[
            pltpu.VMEM((4, tokens, width), BF16),
            pltpu.VMEM((4, tokens, width), BF16),
            pltpu.VMEM((2, tokens, width), F32),
            states, states,
            pltpu.VMEM((heads, sub, HEAD_DIM, HEAD_DIM), BF16),
            state, state, state, state, state, state, state, state,
            pltpu.VMEM((local_heads * HEAD_DIM,), F32),
            pltpu.VMEM((DETOUR_ARRAYS, rows, DETOUR_CHUNKS * step * HEAD_DIM), BF16),
            pltpu.SemaphoreType.DMA((chunks,)), pltpu.SemaphoreType.DMA,
            pltpu.SemaphoreType.REGULAR((3,)),
        ],
        compiler_params=pltpu.CompilerParams(
            collective_id=0, has_side_effects=True, vmem_limit_bytes=51000 * 1024),
    )(query, key, value, cotangent, pltpu.with_memory_space_constraint(gain, pltpu.HBM),
      incoming_state)
    return pl.pallas_call(
        functools.partial(land, 4 if rows % 64 == 0 else 1),
        out_shape=shapes,
        in_specs=[anywhere] * 4,
        out_specs=[anywhere] * 4,
        scratch_shapes=[pltpu.SemaphoreType.DMA],
        compiler_params=pltpu.CompilerParams(vmem_limit_bytes=1024 * 1024),
    )(*results)


def solution(mesh):
    tokens = P(("seq", "head"), None)
    return jax.shard_map(
        functools.partial(per_device, mesh),
        mesh=mesh,
        in_specs=(tokens, tokens, tokens, tokens, P("head"), P("head", None, None)),
        out_specs=(tokens, tokens, tokens, tokens),
        check_vma=False,
    )
```

```python
import functools

import jax
import jax.numpy as jnp
from jax import lax
from jax.experimental import pallas as pl
from jax.experimental.pallas import tpu as pltpu
from jax.sharding import PartitionSpec as P

HEAD_DIM = 128
EPSILON = 1e-06
DETOUR_ARRAYS, DETOUR_CHUNKS = 1, 1
MESH = pl.DeviceIdType.MESH
F32 = jnp.float32
BF16 = jnp.bfloat16

NT = (((1,), (1,)), ((), ()))
TN = (((0,), (0,)), ((), ()))
NN = (((1,), (0,)), ((), ()))


def dot(a, b, dims):
    return lax.dot_general(a, b, dims, preferred_element_type=F32)


def kernel(plan, q_hbm, k_hbm, v_hbm, y_hbm, gain_hbm, s0_hbm, o_out, gq_out, gk_out, gv_out,
           xin, xout, part, cum, gcum, prefix, tot, gtot, xt, xg, pin, psend, sin, ssend, gain, hop,
           first_recv, in_send, entered):
    n_outer, n_inner, sub, n_head, rows, heads, step = plan
    peers = sub * n_head
    chunks = heads // step
    block = rows * n_head
    span = step * HEAD_DIM
    seq, hd = lax.axis_index("seq"), lax.axis_index("head")
    group, j = seq // sub, lax.rem(seq, sub)
    outer, inner = group // n_inner, lax.rem(group, n_inner)
    me = j * n_head + hd

    def place(p):
        to_j = lax.rem(j + p // n_head, sub)
        to_hd = lax.rem(hd + lax.rem(p, n_head), n_head)
        return to_j * n_head + to_hd, (group * sub + to_j, to_hd)

    def column(other, c):
        owner = lax.rem(other, n_head) * (sub * heads) + (other // n_head) * heads + c * step
        return pl.ds(pl.multiple_of(owner * HEAD_DIM, span), span)

    def strip(index):
        return pl.ds(pl.multiple_of(index * rows, rows), rows)

    def cols(c):
        return pl.ds(pl.multiple_of(c * span, span), span)

    def piece(c):
        return pl.ds(c * step, step)

    across = ((outer * n_inner + (n_inner - 1 - inner)) * sub + j, hd)
    later = (seq + n_inner * sub, hd)
    earlier = (seq - n_inner * sub, hd)
    first, last = outer == 0, outer == n_outer - 1
    detours = n_outer > 1 and n_inner == 2 and n_head == 2
    partner = (seq, n_head - 1 - hd)
    by_x = j == 0
    hop_device = (jnp.where(by_x, across[0], later[0]), n_head - 1 - hd)
    owes = jnp.logical_and(group == 0, hd == 1)
    owed = jnp.logical_and(group == 0, hd == 0)
    relays = jnp.logical_and(group == jnp.where(by_x, 1, n_inner), hd == 0)
    passed_to = (jnp.where(by_x, across[0], earlier[0]), hd)
    barrier = pltpu.get_barrier_semaphore()

    def greet(p, carry):
        _, device = place(p)
        pl.semaphore_signal(barrier, inc=1, device_id=device, device_id_type=MESH)
        return carry

    lax.fori_loop(1, peers, greet, 0)
    inside = inner == 0

    if n_inner == 2:
        @pl.when(inside)
        def _():
            pl.semaphore_signal(barrier, inc=1, device_id=across, device_id_type=MESH)

    @pl.when(jnp.logical_not(last))
    def _():
        pl.semaphore_signal(barrier, inc=1, device_id=later, device_id_type=MESH)

    sources = ((k_hbm, v_hbm), (q_hbm, y_hbm))
    targets = ((o_out, gq_out), (gk_out, gv_out))

    for more_x in range(n_inner):
        for more_z in range(2):
            @pl.when(jnp.logical_and(inner == more_x, first == (more_z == 0)))
            def _(more=more_x + more_z):
                pl.semaphore_wait(barrier, peers - 1 + more)

    def scatter(phase, recv):
        def chunk(c, carry):
            def one(p, carry):
                other, device = place(p)
                for a in range(2):
                    pltpu.make_async_remote_copy(
                        src_ref=sources[phase][a].at[:, column(other, c)],
                        dst_ref=xin.at[2 * phase + a, strip(me), cols(c)],
                        send_sem=in_send,
                        recv_sem=recv.at[c],
                        device_id=device,
                        device_id_type=MESH,
                    ).start()
                return carry

            lax.fori_loop(1, peers, one, 0)
            for a in range(2):
                pltpu.make_async_copy(
                    sources[phase][a].at[:, column(me, c)],
                    xin.at[2 * phase + a, strip(me), cols(c)],
                    recv.at[c],
                ).start()
            return carry

        lax.fori_loop(0, chunks, chunk, 0)

    scatter(0, first_recv)

    def rest(second_recv, chain_recv, t_recv, g_recv, out_send, out_recv,
             p_send, s_send, t_send, g_send, gain_sem, hop_send, hop_recv):
        in_recv = first_recv, second_recv

        def announce(p, carry):
            _, device = place(p)
            pl.semaphore_signal(entered.at[0], inc=1, device_id=device, device_id_type=MESH)
            return carry

        lax.fori_loop(1, peers, announce, 0)
        gains = pltpu.make_async_copy(gain_hbm, gain, gain_sem)
        gains.start()

        if n_inner == 2:
            @pl.when(jnp.logical_not(inside))
            def _():
                pl.semaphore_signal(entered.at[0], inc=1, device_id=across, device_id_type=MESH)

        @pl.when(jnp.logical_not(first))
        def _():
            pl.semaphore_signal(entered.at[0], inc=1, device_id=earlier, device_id_type=MESH)

        @pl.when(first)
        def _():
            def carried_in(c, carry):
                pltpu.make_async_copy(
                    s0_hbm.at[pl.ds(j * heads + c * step, step)], pin.at[piece(c)], chain_recv.at[c],
                ).start()
                return carry

            lax.fori_loop(0, chunks, carried_in, 0)

        @pl.when(last)
        def _():
            sin[...] = jnp.zeros_like(sin)

        row = lax.broadcasted_iota(jnp.int32, (block, block), 0)
        col = lax.broadcasted_iota(jnp.int32, (block, block), 1)
        causal = col <= row
        gains.wait()

        for more_x in range(n_inner):
            for more_z in range(2):
                @pl.when(jnp.logical_and(inner == n_inner - 1 - more_x, last == (more_z == 0)))
                def _(more=more_x + more_z):
                    pl.semaphore_wait(entered.at[0], peers - 1 + more)

        if n_inner == 2:
            @pl.when(inside)
            def _():
                pl.semaphore_signal(entered.at[1], inc=1, device_id=across, device_id_type=MESH)

        @pl.when(jnp.logical_not(last))
        def _():
            pl.semaphore_signal(entered.at[1], inc=1, device_id=later, device_id_type=MESH)

        if detours:
            @pl.when(owed)
            def _():
                pl.semaphore_signal(entered.at[2], inc=1, device_id=partner, device_id_type=MESH)

        scatter(1, second_recv)

        for more_x in range(n_inner):
            for more_z in range(2):
                if more_x + more_z > 0:
                    @pl.when(jnp.logical_and(inner == more_x, first == (more_z == 0)))
                    def _(more=more_x + more_z):
                        pl.semaphore_wait(entered.at[1], more)

        if detours:
            @pl.when(owes)
            def _():
                pl.semaphore_wait(entered.at[2], 1)

        def arrived(phase, c):
            ref = xin.at[pl.ds(2 * phase, 2), :, cols(c)]
            pltpu.make_async_copy(ref, ref, in_recv[phase].at[c]).wait()

        def give(phase, c):
            def back(p, carry):
                other, device = place(p)
                for a in range(2):
                    def send(dst, device, recv, a=a):
                        pltpu.make_async_remote_copy(
                            src_ref=xout.at[2 * phase + a, strip(other), cols(c)], dst_ref=dst,
                            send_sem=out_send, recv_sem=recv, device_id=device, device_id_type=MESH,
                        ).start()

                    target = targets[phase][a].at[:, column(me, c)]
                    if detours and phase == 0 and a < DETOUR_ARRAYS:
                        detour = jnp.logical_and(owes, jnp.logical_and(c < DETOUR_CHUNKS, p == 1))

                        @pl.when(detour)
                        def _():
                            send(hop.at[a, :, cols(c)], hop_device, hop_recv)

                        @pl.when(jnp.logical_not(detour))
                        def _():
                            send(target, device, out_recv)
                    else:
                        send(target, device, out_recv)
                return carry

            lax.fori_loop(1, peers, back, 0)
            for a in range(2):
                pltpu.make_async_copy(
                    xout.at[2 * phase + a, strip(me), cols(c)],
                    targets[phase][a].at[:, column(me, c)],
                    out_recv,
                ).start()

        def state_copy(src, dst, send, recv, c, device):
            return pltpu.make_async_remote_copy(
                src_ref=src.at[piece(c)], dst_ref=dst.at[piece(c)], send_sem=send,
                recv_sem=recv.at[c], device_id=device, device_id_type=MESH)

        def landed(ref, recv, c):
            pltpu.make_async_copy(ref.at[piece(c)], ref.at[piece(c)], recv.at[c]).wait()

        def lanes(c, h):
            return pl.ds(pl.multiple_of(c * span + h * HEAD_DIM, HEAD_DIM), HEAD_DIM)

        def block_states(c):
            arrived(0, c)
            for h in range(step):
                n, hc = c * step + h, lanes(c, h)
                run = dot(xin[0, :block, hc], xin[1, :block, hc], TN)
                for b in range(1, sub):
                    r = slice(b * block, (b + 1) * block)
                    cum[n, b - 1] = run
                    run = run + dot(xin[0, r, hc], xin[1, r, hc], TN)
                tot[n] = run
            if n_inner == 2:
                state_copy(tot, xt, t_send, t_recv, c, across).start()

        def pass_prefix(c):
            if n_inner == 2:
                landed(xt, t_recv, c)
            landed(pin, chain_recv, c)

            @pl.when(jnp.logical_not(last))
            def _():
                for h in range(step):
                    n = c * step + h
                    psend[n] = pin[n] + tot[n] + xt[n] if n_inner == 2 else pin[n] + tot[n]
                state_copy(psend, pin, p_send, chain_recv, c, later).start()

            for h in range(step):
                n = c * step + h
                before = pin[n]
                if n_inner == 2:
                    before = before + jnp.where(inner == 1, xt[n], 0.0)
                prefix[n, 0] = before.astype(BF16)
                for b in range(1, sub):
                    prefix[n, b] = (before + cum[n, b - 1]).astype(BF16)

        def attend(c):
            arrived(1, c)
            for h in range(step):
                n, hc = c * step + h, lanes(c, h)
                at = pl.multiple_of((j * heads + n) * HEAD_DIM, HEAD_DIM)
                g = gain[pl.ds(at, HEAD_DIM)].reshape(1, HEAD_DIM)
                run = None
                for b in reversed(range(sub)):
                    r = slice(b * block, (b + 1) * block)
                    k, v, q, up = xin[0, r, hc], xin[1, r, hc], xin[2, r, hc], xin[3, r, hc]
                    state = prefix[n, b]
                    w = jnp.where(causal, dot(q, k, NT), 0.0).astype(BF16)
                    att = dot(w, v, NN) + dot(q, state, NN)
                    inv = lax.rsqrt(jnp.mean(att * att, axis=-1, keepdims=True) + EPSILON)
                    normed = att * inv
                    xout[0, r, hc] = (normed * g).astype(BF16)
                    scaled = up.astype(F32) * g
                    ga = ((scaled - normed * jnp.mean(scaled * normed, axis=-1, keepdims=True))
                          * inv).astype(BF16)
                    gw = jnp.where(causal, dot(ga, v, NT), 0.0).astype(BF16)
                    xout[1, r, hc] = (dot(gw, k, NN) + dot(ga, state, NT)).astype(BF16)
                    part[0, r, hc] = dot(gw, q, TN)
                    part[1, r, hc] = dot(w, ga, TN)
                    if run is not None:
                        gcum[n, b] = run
                    grad = dot(q, ga, TN)
                    run = grad if run is None else run + grad
                gtot[n] = run
            if n_inner == 2:
                state_copy(gtot, xg, g_send, g_recv, c, across).start()
            give(0, c)

        def finish(c):
            if n_inner == 2:
                landed(xg, g_recv, c)

            @pl.when(jnp.logical_not(last))
            def _():
                landed(sin, chain_recv, c)

            @pl.when(jnp.logical_not(first))
            def _():
                for h in range(step):
                    n = c * step + h
                    ssend[n] = sin[n] + gtot[n] + xg[n] if n_inner == 2 else sin[n] + gtot[n]
                state_copy(ssend, sin, s_send, chain_recv, c, earlier).start()

            for h in range(step):
                n, hc = c * step + h, lanes(c, h)
                after = sin[n]
                if n_inner == 2:
                    after = after + jnp.where(inner == 0, xg[n], 0.0)
                for b in range(sub):
                    r = slice(b * block, (b + 1) * block)
                    suffix = (after + gcum[n, b] if b < sub - 1 else after).astype(BF16)
                    xout[2, r, hc] = (part[0, r, hc] + dot(xin[1, r, hc], suffix, NT)).astype(BF16)
                    xout[3, r, hc] = (part[1, r, hc] + dot(xin[0, r, hc], suffix, NN)).astype(BF16)
            give(1, c)

        prefix_lag = jnp.minimum(2 + 2 * outer, chunks)
        suffix_lag = chunks + 2 + 2 * (n_outer - 1 - outer)

        def tick(i, carry):
            @pl.when(i < chunks)
            def _():
                block_states(i)

            @pl.when(jnp.logical_and(i >= prefix_lag, i < prefix_lag + chunks))
            def _():
                pass_prefix(i - prefix_lag)

            @pl.when(jnp.logical_and(i >= chunks, i < 2 * chunks))
            def _():
                attend(i - chunks)

            @pl.when(jnp.logical_and(i >= suffix_lag, i < suffix_lag + chunks))
            def _():
                finish(i - suffix_lag)

            return carry

        lax.fori_loop(0, 2 * chunks + 2 * n_outer, tick, 0)

        if detours:
            @pl.when(relays)
            def _():
                pltpu.make_async_copy(hop, hop, hop_recv).wait()
                whole = pl.ds(pl.multiple_of((sub * heads + j * heads) * HEAD_DIM, span), hop.shape[2])
                for a in range(DETOUR_ARRAYS):
                    pltpu.make_async_remote_copy(
                        src_ref=hop.at[a], dst_ref=targets[0][a].at[:, whole], send_sem=hop_send,
                        recv_sem=out_recv, device_id=passed_to, device_id_type=MESH).start()
                pltpu.make_async_copy(hop, hop, hop_send).wait()

        sent = xin.at[:, pl.ds(0, (peers - 1) * rows)]
        pltpu.make_async_copy(sent, sent, in_send).wait()
        pltpu.make_async_copy(sent, sent, out_send).wait()
        if n_inner == 2:
            pltpu.make_async_copy(tot, tot, t_send).wait()
            pltpu.make_async_copy(gtot, gtot, g_send).wait()

        @pl.when(jnp.logical_not(last))
        def _():
            pltpu.make_async_copy(psend, psend, p_send).wait()

        @pl.when(jnp.logical_not(first))
        def _():
            pltpu.make_async_copy(ssend, ssend, s_send).wait()

        pltpu.make_async_copy(xout, xout, out_recv).wait()

    one = pltpu.SemaphoreType.DMA
    chain = one((chunks,))
    pl.run_scoped(rest, chain, chain, chain, chain, *[one] * 9)


def land(parts, *refs):
    sources, targets, sem = refs[:4], refs[4:8], refs[8]
    copies = []
    rows = sources[0].shape[0] // parts
    for part in range(parts):
        for src, dst in zip(sources, targets):
            piece = pl.ds(part * rows, rows)
            copies.append(pltpu.make_async_copy(src.at[piece], dst.at[piece], sem))
            copies[-1].start()
    for copy in copies:
        copy.wait()


def per_device(mesh, query, key, value, cotangent, gain, incoming_state):
    n_seq, n_head = mesh.shape["seq"], mesh.shape["head"]
    rows, features = query.shape
    local_heads = incoming_state.shape[0]
    sub = 2 if n_seq % 2 == 0 and local_heads % 2 == 0 else 1
    n_inner = 2 if n_seq % (2 * sub) == 0 else 1
    n_outer = n_seq // (sub * n_inner)
    heads = local_heads // sub
    step = next(s for s in range(max(1, heads // 8), heads + 1) if heads % s == 0)
    chunks = heads // step
    tokens = rows * n_head * sub
    width = heads * HEAD_DIM
    plan = (n_outer, n_inner, sub, n_head, rows, heads, step)
    anywhere = pl.BlockSpec(memory_space=pl.ANY)
    resident = pl.BlockSpec(memory_space=pltpu.HBM)
    state = pltpu.VMEM((heads, HEAD_DIM, HEAD_DIM), F32)
    states = pltpu.VMEM((heads, max(1, sub - 1), HEAD_DIM, HEAD_DIM), F32)
    shapes = [jax.ShapeDtypeStruct((rows, features), BF16)] * 4
    results = pl.pallas_call(
        functools.partial(kernel, plan),
        out_shape=shapes,
        in_specs=[resident] * 6,
        out_specs=[anywhere] * 4,
        scratch_shapes=[
            pltpu.VMEM((4, tokens, width), BF16),
            pltpu.VMEM((4, tokens, width), BF16),
            pltpu.VMEM((2, tokens, width), F32),
            states, states,
            pltpu.VMEM((heads, sub, HEAD_DIM, HEAD_DIM), BF16),
            state, state, state, state, state, state, state, state,
            pltpu.VMEM((local_heads * HEAD_DIM,), F32),
            pltpu.VMEM((DETOUR_ARRAYS, rows, DETOUR_CHUNKS * step * HEAD_DIM), BF16),
            pltpu.SemaphoreType.DMA((chunks,)), pltpu.SemaphoreType.DMA,
            pltpu.SemaphoreType.REGULAR((3,)),
        ],
        compiler_params=pltpu.CompilerParams(
            collective_id=0, has_side_effects=True, vmem_limit_bytes=51000 * 1024),
    )(query, key, value, cotangent, pltpu.with_memory_space_constraint(gain, pltpu.HBM),
      incoming_state)
    return pl.pallas_call(
        functools.partial(land, 4 if rows % 64 == 0 else 1),
        out_shape=shapes,
        in_specs=[anywhere] * 4,
        out_specs=[anywhere] * 4,
        scratch_shapes=[pltpu.SemaphoreType.DMA],
        compiler_params=pltpu.CompilerParams(vmem_limit_bytes=1024 * 1024),
    )(*results)


def solution(mesh):
    tokens = P(("seq", "head"), None)
    return jax.shard_map(
        functools.partial(per_device, mesh),
        mesh=mesh,
        in_specs=(tokens, tokens, tokens, tokens, P("head"), P("head", None, None)),
        out_specs=(tokens, tokens, tokens, tokens),
        check_vma=False,
    )
```

```python
import functools

import jax
import jax.numpy as jnp
from jax import lax
from jax.experimental import pallas as pl
from jax.experimental.pallas import tpu as pltpu
from jax.sharding import PartitionSpec as P

HEAD_DIM = 128
EPSILON = 1e-06
VMEM = 36000 * 1024
DETOUR_ARRAYS, DETOUR_CHUNKS = 1, 1
MESH = pl.DeviceIdType.MESH
F32 = jnp.float32
BF16 = jnp.bfloat16

NT = (((1,), (1,)), ((), ()))
TN = (((0,), (0,)), ((), ()))
NN = (((1,), (0,)), ((), ()))


def dot(a, b, dims):
    return lax.dot_general(a, b, dims, preferred_element_type=F32)


def kernel(plan, q_hbm, k_hbm, v_hbm, y_hbm, gain_hbm, s0_hbm, o_out, gq_out, gk_out, gv_out,
           hold, tail, xin, xout, part, cum, gcum, prefix, tot, gtot, xt, xg, pin, psend, sin, ssend, gain, hop,
           first_recv, in_send, entered):
    n_outer, n_inner, sub, n_head, rows, heads, step, late = plan
    peers = sub * n_head
    chunks = heads // step
    block = rows * n_head
    span = step * HEAD_DIM
    seq, hd = lax.axis_index("seq"), lax.axis_index("head")
    group, j = seq // sub, lax.rem(seq, sub)
    outer, inner = group // n_inner, lax.rem(group, n_inner)
    me = j * n_head + hd

    def place(p):
        to_j = lax.rem(j + p // n_head, sub)
        to_hd = lax.rem(hd + lax.rem(p, n_head), n_head)
        return to_j * n_head + to_hd, (group * sub + to_j, to_hd)

    def column(other, c):
        owner = lax.rem(other, n_head) * (sub * heads) + (other // n_head) * heads + c * step
        return pl.ds(pl.multiple_of(owner * HEAD_DIM, span), span)

    def strip(index):
        return pl.ds(pl.multiple_of(index * rows, rows), rows)

    def cols(c):
        return pl.ds(pl.multiple_of(c * span, span), span)

    def piece(c):
        return pl.ds(c * step, step)

    across = ((outer * n_inner + (n_inner - 1 - inner)) * sub + j, hd)
    later = (seq + n_inner * sub, hd)
    earlier = (seq - n_inner * sub, hd)
    first, last = outer == 0, outer == n_outer - 1
    detours = n_outer > 1 and n_inner == 2 and n_head == 2
    partner = (seq, n_head - 1 - hd)
    by_x = j == 0
    hop_device = (jnp.where(by_x, across[0], later[0]), n_head - 1 - hd)
    owes = jnp.logical_and(group == 0, hd == 1)
    owed = jnp.logical_and(group == 0, hd == 0)
    relays = jnp.logical_and(group == jnp.where(by_x, 1, n_inner), hd == 0)
    passed_to = (jnp.where(by_x, across[0], earlier[0]), hd)
    barrier = pltpu.get_barrier_semaphore()

    def greet(p, carry):
        _, device = place(p)
        pl.semaphore_signal(barrier, inc=1, device_id=device, device_id_type=MESH)
        return carry

    lax.fori_loop(1, peers, greet, 0)
    inside = inner == 0

    if n_inner == 2:
        @pl.when(inside)
        def _():
            pl.semaphore_signal(barrier, inc=1, device_id=across, device_id_type=MESH)

    @pl.when(jnp.logical_not(last))
    def _():
        pl.semaphore_signal(barrier, inc=1, device_id=later, device_id_type=MESH)

    sources = ((k_hbm, v_hbm), (q_hbm, y_hbm))
    targets = ((o_out, gq_out), (gk_out, gv_out))

    for more_x in range(n_inner):
        for more_z in range(2):
            @pl.when(jnp.logical_and(inner == more_x, first == (more_z == 0)))
            def _(more=more_x + more_z):
                pl.semaphore_wait(barrier, peers - 1 + more)

    def scatter(phase, recv):
        def chunk(c, carry):
            def one(p, carry):
                other, device = place(p)
                for a in range(2):
                    pltpu.make_async_remote_copy(
                        src_ref=sources[phase][a].at[:, column(other, c)],
                        dst_ref=xin.at[2 * phase + a, strip(me), cols(c)],
                        send_sem=in_send,
                        recv_sem=recv.at[c],
                        device_id=device,
                        device_id_type=MESH,
                    ).start()
                return carry

            lax.fori_loop(1, peers, one, 0)
            for a in range(2):
                pltpu.make_async_copy(
                    sources[phase][a].at[:, column(me, c)],
                    xin.at[2 * phase + a, strip(me), cols(c)],
                    recv.at[c],
                ).start()
            return carry

        lax.fori_loop(0, chunks, chunk, 0)

    scatter(0, first_recv)

    def rest(second_recv, chain_recv, t_recv, g_recv, out_send, out_recv,
             p_send, s_send, t_send, g_send, gain_sem, hop_send, hop_recv, own_sem, hold_sem,
             tail_send, tail_recv):
        in_recv = first_recv, second_recv

        def announce(p, carry):
            _, device = place(p)
            pl.semaphore_signal(entered.at[0], inc=1, device_id=device, device_id_type=MESH)
            return carry

        lax.fori_loop(1, peers, announce, 0)
        gains = pltpu.make_async_copy(gain_hbm, gain, gain_sem)
        gains.start()

        if n_inner == 2:
            @pl.when(jnp.logical_not(inside))
            def _():
                pl.semaphore_signal(entered.at[0], inc=1, device_id=across, device_id_type=MESH)

        @pl.when(jnp.logical_not(first))
        def _():
            pl.semaphore_signal(entered.at[0], inc=1, device_id=earlier, device_id_type=MESH)

        @pl.when(first)
        def _():
            def carried_in(c, carry):
                pltpu.make_async_copy(
                    s0_hbm.at[pl.ds(j * heads + c * step, step)], pin.at[piece(c)], chain_recv.at[c],
                ).start()
                return carry

            lax.fori_loop(0, chunks, carried_in, 0)

        @pl.when(last)
        def _():
            sin[...] = jnp.zeros_like(sin)

        row = lax.broadcasted_iota(jnp.int32, (block, block), 0)
        col = lax.broadcasted_iota(jnp.int32, (block, block), 1)
        causal = col <= row
        gains.wait()

        for more_x in range(n_inner):
            for more_z in range(2):
                @pl.when(jnp.logical_and(inner == n_inner - 1 - more_x, last == (more_z == 0)))
                def _(more=more_x + more_z):
                    pl.semaphore_wait(entered.at[0], peers - 1 + more)

        if n_inner == 2:
            @pl.when(inside)
            def _():
                pl.semaphore_signal(entered.at[1], inc=1, device_id=across, device_id_type=MESH)

        @pl.when(jnp.logical_not(last))
        def _():
            pl.semaphore_signal(entered.at[1], inc=1, device_id=later, device_id_type=MESH)

        if detours:
            @pl.when(owed)
            def _():
                pl.semaphore_signal(entered.at[2], inc=1, device_id=partner, device_id_type=MESH)

        scatter(1, second_recv)

        for more_x in range(n_inner):
            for more_z in range(2):
                if more_x + more_z > 0:
                    @pl.when(jnp.logical_and(inner == more_x, first == (more_z == 0)))
                    def _(more=more_x + more_z):
                        pl.semaphore_wait(entered.at[1], more)

        if detours:
            @pl.when(owes)
            def _():
                pl.semaphore_wait(entered.at[2], 1)

        def arrived(phase, c):
            ref = xin.at[pl.ds(2 * phase, 2), :, cols(c)]
            pltpu.make_async_copy(ref, ref, in_recv[phase].at[c]).wait()

        def give(phase, c):
            def back(p, carry):
                other, device = place(p)
                for a in range(2):
                    def send(dst, device, recv, a=a):
                        pltpu.make_async_remote_copy(
                            src_ref=xout.at[2 * phase + a, strip(other), cols(c)], dst_ref=dst,
                            send_sem=out_send, recv_sem=recv, device_id=device, device_id_type=MESH,
                        ).start()

                    target = targets[phase][a].at[:, column(me, c)]
                    if detours and phase == 0 and a < DETOUR_ARRAYS:
                        detour = jnp.logical_and(owes, jnp.logical_and(c < DETOUR_CHUNKS, p == 1))

                        @pl.when(detour)
                        def _():
                            send(hop.at[a, :, cols(c)], hop_device, hop_recv)

                        @pl.when(jnp.logical_not(detour))
                        def _():
                            send(target, device, out_recv)
                    elif late and phase == 1:
                        held = jnp.logical_and(p == 1, c >= chunks - late)

                        @pl.when(held)
                        def _(a=a):
                            at = pl.multiple_of((c - (chunks - late)) * span, span)
                            pltpu.make_async_copy(
                                xout.at[2 + a, strip(other), cols(c)],
                                hold.at[a, :, pl.ds(at, span)], hold_sem).start()

                        @pl.when(jnp.logical_not(held))
                        def _():
                            send(target, device, out_recv)
                    else:
                        send(target, device, out_recv)
                return carry

            lax.fori_loop(1, peers, back, 0)
            for a in range(2):
                pltpu.make_async_copy(
                    xout.at[2 * phase + a, strip(me), cols(c)],
                    targets[phase][a].at[:, column(me, c)],
                    own_sem,
                ).start()

        def state_copy(src, dst, send, recv, c, device):
            return pltpu.make_async_remote_copy(
                src_ref=src.at[piece(c)], dst_ref=dst.at[piece(c)], send_sem=send,
                recv_sem=recv.at[c], device_id=device, device_id_type=MESH)

        def landed(ref, recv, c):
            pltpu.make_async_copy(ref.at[piece(c)], ref.at[piece(c)], recv.at[c]).wait()

        def lanes(c, h):
            return pl.ds(pl.multiple_of(c * span + h * HEAD_DIM, HEAD_DIM), HEAD_DIM)

        def block_states(c):
            arrived(0, c)
            for h in range(step):
                n, hc = c * step + h, lanes(c, h)
                run = dot(xin[0, :block, hc], xin[1, :block, hc], TN)
                for b in range(1, sub):
                    r = slice(b * block, (b + 1) * block)
                    cum[n, b - 1] = run
                    run = run + dot(xin[0, r, hc], xin[1, r, hc], TN)
                tot[n] = run
            if n_inner == 2:
                state_copy(tot, xt, t_send, t_recv, c, across).start()

        def pass_prefix(c):
            if n_inner == 2:
                landed(xt, t_recv, c)
            landed(pin, chain_recv, c)

            @pl.when(jnp.logical_not(last))
            def _():
                for h in range(step):
                    n = c * step + h
                    psend[n] = pin[n] + tot[n] + xt[n] if n_inner == 2 else pin[n] + tot[n]
                state_copy(psend, pin, p_send, chain_recv, c, later).start()

            for h in range(step):
                n = c * step + h
                before = pin[n]
                if n_inner == 2:
                    before = before + jnp.where(inner == 1, xt[n], 0.0)
                prefix[n, 0] = before.astype(BF16)
                for b in range(1, sub):
                    prefix[n, b] = (before + cum[n, b - 1]).astype(BF16)

        def attend(c):
            arrived(1, c)
            for h in range(step):
                n, hc = c * step + h, lanes(c, h)
                at = pl.multiple_of((j * heads + n) * HEAD_DIM, HEAD_DIM)
                g = gain[pl.ds(at, HEAD_DIM)].reshape(1, HEAD_DIM)
                run = None
                for b in reversed(range(sub)):
                    r = slice(b * block, (b + 1) * block)
                    k, v, q, up = xin[0, r, hc], xin[1, r, hc], xin[2, r, hc], xin[3, r, hc]
                    state = prefix[n, b]
                    w = jnp.where(causal, dot(q, k, NT), 0.0).astype(BF16)
                    att = dot(w, v, NN) + dot(q, state, NN)
                    inv = lax.rsqrt(jnp.mean(att * att, axis=-1, keepdims=True) + EPSILON)
                    normed = att * inv
                    xout[0, r, hc] = (normed * g).astype(BF16)
                    scaled = up.astype(F32) * g
                    ga = ((scaled - normed * jnp.mean(scaled * normed, axis=-1, keepdims=True))
                          * inv).astype(BF16)
                    gw = jnp.where(causal, dot(ga, v, NT), 0.0).astype(BF16)
                    xout[1, r, hc] = (dot(gw, k, NN) + dot(ga, state, NT)).astype(BF16)
                    part[0, r, hc] = dot(gw, q, TN)
                    part[1, r, hc] = dot(w, ga, TN)
                    if run is not None:
                        gcum[n, b] = run
                    grad = dot(q, ga, TN)
                    run = grad if run is None else run + grad
                gtot[n] = run
            if n_inner == 2:
                state_copy(gtot, xg, g_send, g_recv, c, across).start()
            give(0, c)

        def finish(c):
            if n_inner == 2:
                landed(xg, g_recv, c)

            @pl.when(jnp.logical_not(last))
            def _():
                landed(sin, chain_recv, c)

            @pl.when(jnp.logical_not(first))
            def _():
                for h in range(step):
                    n = c * step + h
                    ssend[n] = sin[n] + gtot[n] + xg[n] if n_inner == 2 else sin[n] + gtot[n]
                state_copy(ssend, sin, s_send, chain_recv, c, earlier).start()

            for h in range(step):
                n, hc = c * step + h, lanes(c, h)
                after = sin[n]
                if n_inner == 2:
                    after = after + jnp.where(inner == 0, xg[n], 0.0)
                for b in range(sub):
                    r = slice(b * block, (b + 1) * block)
                    suffix = (after + gcum[n, b] if b < sub - 1 else after).astype(BF16)
                    xout[2, r, hc] = (part[0, r, hc] + dot(xin[1, r, hc], suffix, NT)).astype(BF16)
                    xout[3, r, hc] = (part[1, r, hc] + dot(xin[0, r, hc], suffix, NN)).astype(BF16)
            give(1, c)

        prefix_lag = jnp.minimum(2 + 2 * outer, chunks)
        suffix_lag = chunks + 2 + 2 * (n_outer - 1 - outer)

        def tick(i, carry):
            @pl.when(i < chunks)
            def _():
                block_states(i)

            @pl.when(jnp.logical_and(i >= prefix_lag, i < prefix_lag + chunks))
            def _():
                pass_prefix(i - prefix_lag)

            @pl.when(jnp.logical_and(i >= chunks, i < 2 * chunks))
            def _():
                attend(i - chunks)

            @pl.when(jnp.logical_and(i >= suffix_lag, i < suffix_lag + chunks))
            def _():
                finish(i - suffix_lag)

            return carry

        lax.fori_loop(0, 2 * chunks + 2 * n_outer, tick, 0)

        if detours:
            @pl.when(relays)
            def _():
                pltpu.make_async_copy(hop, hop, hop_recv).wait()
                whole = pl.ds(pl.multiple_of((sub * heads + j * heads) * HEAD_DIM, span), hop.shape[2])
                for a in range(DETOUR_ARRAYS):
                    pltpu.make_async_remote_copy(
                        src_ref=hop.at[a], dst_ref=targets[0][a].at[:, whole], send_sem=hop_send,
                        recv_sem=out_recv, device_id=passed_to, device_id_type=MESH).start()
                pltpu.make_async_copy(hop, hop, hop_send).wait()

        sent = xin.at[:, pl.ds(0, (peers - 1) * rows)]
        back = xin.at[:, :, pl.ds(0, 5 * chunks // 8 * span)] if late else sent
        mine = xin.at[:, pl.ds(0, rows)]
        if late:
            to_partner = pltpu.make_async_remote_copy(
                src_ref=hold, dst_ref=tail, send_sem=tail_send, recv_sem=tail_recv,
                device_id=partner, device_id_type=MESH)
            pltpu.make_async_copy(hold, hold, hold_sem).wait()

            @pl.when(j == sub - 1)
            def _():
                to_partner.start()

        pltpu.make_async_copy(sent, sent, in_send).wait()
        pltpu.make_async_copy(back, back, out_send).wait()
        pltpu.make_async_copy(mine, mine, own_sem).wait()
        if n_inner == 2:
            pltpu.make_async_copy(tot, tot, t_send).wait()
            pltpu.make_async_copy(gtot, gtot, g_send).wait()

        @pl.when(jnp.logical_not(last))
        def _():
            pltpu.make_async_copy(psend, psend, p_send).wait()

        @pl.when(jnp.logical_not(first))
        def _():
            pltpu.make_async_copy(ssend, ssend, s_send).wait()

        pltpu.make_async_copy(back, back, out_recv).wait()
        if late:
            @pl.when(j == sub - 1)
            def _():
                to_partner.wait()

    one = pltpu.SemaphoreType.DMA
    chain = one((chunks,))
    pl.run_scoped(rest, chain, chain, chain, chain, *[one] * 13)


def land(*refs):
    sources, targets, sem = refs[:4], refs[-5:-1], refs[-1]
    copies = [pltpu.make_async_copy(src, dst, sem) for src, dst in zip(sources, targets)]
    for copy in copies:
        copy.start()
    for copy in copies:
        copy.wait()


def last_pieces(sub, hold, tail, written, out, sem, send, recv):
    seq, hd = lax.axis_index("seq"), lax.axis_index("head")
    partner = (seq, 1 - hd)
    barrier = pltpu.get_barrier_semaphore()

    @pl.when(lax.rem(seq, sub) < sub - 1)
    def _():
        pl.semaphore_signal(barrier, inc=1, device_id=partner, device_id_type=MESH)
        pl.semaphore_wait(barrier, 1)
        copy = pltpu.make_async_remote_copy(
            src_ref=hold, dst_ref=out, send_sem=send, recv_sem=recv,
            device_id=partner, device_id_type=MESH)
        copy.start()
        copy.wait()

    @pl.when(lax.rem(seq, sub) == sub - 1)
    def _():
        copy = pltpu.make_async_copy(tail, out, sem)
        copy.start()
        copy.wait()


def land_last(plan, tail, gk_in, gv_in, gk_out, gv_out, sem):
    n_outer, n_inner, sub, n_head, rows, heads, step, late = plan
    seq, hd = lax.axis_index("seq"), lax.axis_index("head")
    first = (1 - hd) * (sub * heads) + lax.rem(seq, sub) * heads + heads - late * step
    at = pl.ds(pl.multiple_of(first * HEAD_DIM, HEAD_DIM), late * step * HEAD_DIM)
    copies = [pltpu.make_async_copy(tail.at[a], out.at[:, at], sem)
              for a, out in enumerate((gk_out, gv_out))]
    for copy in copies:
        copy.start()
    for copy in copies:
        copy.wait()


def per_device(mesh, query, key, value, cotangent, gain, incoming_state):
    n_seq, n_head = mesh.shape["seq"], mesh.shape["head"]
    rows, features = query.shape
    local_heads = incoming_state.shape[0]
    sub = 2 if n_seq % 2 == 0 and local_heads % 2 == 0 else 1
    n_inner = 2 if n_seq % (2 * sub) == 0 else 1
    n_outer = n_seq // (sub * n_inner)
    heads = local_heads // sub
    step = next(s for s in range(max(1, heads // 8), heads + 1) if heads % s == 0)
    chunks = heads // step
    tokens = rows * n_head * sub
    width = heads * HEAD_DIM
    splits = sub == 2 and n_head == 2 and n_inner == 2 and n_outer > 1 and chunks % 8 == 0
    late = chunks if splits else 0
    plan = (n_outer, n_inner, sub, n_head, rows, heads, step, late)
    anywhere = pl.BlockSpec(memory_space=pl.ANY)
    resident = pl.BlockSpec(memory_space=pltpu.HBM)
    state = pltpu.VMEM((heads, HEAD_DIM, HEAD_DIM), F32)
    states = pltpu.VMEM((heads, max(1, sub - 1), HEAD_DIM, HEAD_DIM), F32)
    shapes = [jax.ShapeDtypeStruct((rows, features), BF16)] * 4
    pieces = [jax.ShapeDtypeStruct((2, rows, max(1, late) * step * HEAD_DIM), BF16)] * 2
    *results, hold, tail = pl.pallas_call(
        functools.partial(kernel, plan),
        out_shape=shapes + pieces,
        in_specs=[resident] * 6,
        out_specs=[anywhere] * 6,
        scratch_shapes=[
            pltpu.VMEM((4, tokens, width), BF16),
            pltpu.VMEM((4, tokens, width), BF16),
            pltpu.VMEM((2, tokens, width), F32),
            states, states,
            pltpu.VMEM((heads, sub, HEAD_DIM, HEAD_DIM), BF16),
            state, state, state, state, state, state, state, state,
            pltpu.VMEM((local_heads * HEAD_DIM,), F32),
            pltpu.VMEM((DETOUR_ARRAYS, rows, DETOUR_CHUNKS * step * HEAD_DIM), BF16),
            pltpu.SemaphoreType.DMA((chunks,)), pltpu.SemaphoreType.DMA,
            pltpu.SemaphoreType.REGULAR((3,)),
        ],
        compiler_params=pltpu.CompilerParams(
            collective_id=0, has_side_effects=True, vmem_limit_bytes=VMEM),
    )(*(pltpu.with_memory_space_constraint(x, pltpu.HBM)
        for x in (query, key, value, cotangent, gain, incoming_state)))
    small = pltpu.CompilerParams(vmem_limit_bytes=1024 * 1024)
    written = pl.pallas_call(
        land,
        out_shape=shapes,
        in_specs=[anywhere] * 4,
        out_specs=[anywhere] * 4,
        scratch_shapes=[pltpu.SemaphoreType.DMA],
        compiler_params=small,
    )(*results)
    if not late:
        return tuple(written)
    output, grad_query, grad_key, grad_value = written
    tail = pl.pallas_call(
        functools.partial(last_pieces, sub),
        out_shape=pieces[0],
        in_specs=[anywhere] * 3,
        out_specs=anywhere,
        scratch_shapes=[pltpu.SemaphoreType.DMA] * 3,
        compiler_params=pltpu.CompilerParams(
            collective_id=1, has_side_effects=True, vmem_limit_bytes=1024 * 1024),
    )(hold, tail, pltpu.with_memory_space_constraint(grad_key, pltpu.HBM))
    grad_key, grad_value = pl.pallas_call(
        functools.partial(land_last, plan),
        out_shape=shapes[:2],
        in_specs=[anywhere] * 3,
        out_specs=[anywhere] * 2,
        input_output_aliases={1: 0, 2: 1},
        scratch_shapes=[pltpu.SemaphoreType.DMA],
        compiler_params=small,
    )(tail, grad_key, grad_value)
    return output, grad_query, grad_key, grad_value


def solution(mesh):
    tokens = P(("seq", "head"), None)
    return jax.shard_map(
        functools.partial(per_device, mesh),
        mesh=mesh,
        in_specs=(tokens, tokens, tokens, tokens, P("head"), P("head", None, None)),
        out_specs=(tokens, tokens, tokens, tokens),
        check_vma=False,
    )
```

```python
import functools

import jax
import jax.numpy as jnp
from jax import lax
from jax.experimental import pallas as pl
from jax.experimental.pallas import tpu as pltpu
from jax.sharding import PartitionSpec as P

HEAD_DIM = 128
EPSILON = 1e-06
VMEM = 36000 * 1024
DETOUR_ARRAYS, DETOUR_CHUNKS = 1, 1
MESH = pl.DeviceIdType.MESH
F32 = jnp.float32
BF16 = jnp.bfloat16

NT = (((1,), (1,)), ((), ()))
TN = (((0,), (0,)), ((), ()))
NN = (((1,), (0,)), ((), ()))


def dot(a, b, dims):
    return lax.dot_general(a, b, dims, preferred_element_type=F32)


def kernel(plan, q_hbm, k_hbm, v_hbm, y_hbm, gain_hbm, s0_hbm, o_out, gq_out, gk_out, gv_out,
           hold, tail, xin, xout, part, cum, gcum, prefix, tot, gtot, xt, xg, pin, psend, sin, ssend, gain, hop,
           first_recv, in_send, entered):
    n_outer, n_inner, sub, n_head, rows, heads, step, late = plan
    peers = sub * n_head
    chunks = heads // step
    block = rows * n_head
    span = step * HEAD_DIM
    seq, hd = lax.axis_index("seq"), lax.axis_index("head")
    group, j = seq // sub, lax.rem(seq, sub)
    outer, inner = group // n_inner, lax.rem(group, n_inner)
    me = j * n_head + hd

    def place(p):
        to_j = lax.rem(j + p // n_head, sub)
        to_hd = lax.rem(hd + lax.rem(p, n_head), n_head)
        return to_j * n_head + to_hd, (group * sub + to_j, to_hd)

    def column(other, c):
        owner = lax.rem(other, n_head) * (sub * heads) + (other // n_head) * heads + c * step
        return pl.ds(pl.multiple_of(owner * HEAD_DIM, span), span)

    def strip(index):
        return pl.ds(pl.multiple_of(index * rows, rows), rows)

    def cols(c):
        return pl.ds(pl.multiple_of(c * span, span), span)

    def piece(c):
        return pl.ds(c * step, step)

    across = ((outer * n_inner + (n_inner - 1 - inner)) * sub + j, hd)
    later = (seq + n_inner * sub, hd)
    earlier = (seq - n_inner * sub, hd)
    first, last = outer == 0, outer == n_outer - 1
    detours = n_outer > 1 and n_inner == 2 and n_head == 2
    partner = (seq, n_head - 1 - hd)
    by_x = j == 0
    hop_device = (jnp.where(by_x, across[0], later[0]), n_head - 1 - hd)
    owes = group == 0
    relays = group == jnp.where(by_x, 1, n_inner)
    passed_to = (jnp.where(by_x, across[0], earlier[0]), hd)
    barrier = pltpu.get_barrier_semaphore()

    def greet(p, carry):
        _, device = place(p)
        pl.semaphore_signal(barrier, inc=1, device_id=device, device_id_type=MESH)
        return carry

    lax.fori_loop(1, peers, greet, 0)
    inside = inner == 0

    if n_inner == 2:
        @pl.when(inside)
        def _():
            pl.semaphore_signal(barrier, inc=1, device_id=across, device_id_type=MESH)

    @pl.when(jnp.logical_not(last))
    def _():
        pl.semaphore_signal(barrier, inc=1, device_id=later, device_id_type=MESH)

    sources = ((k_hbm, v_hbm), (q_hbm, y_hbm))
    targets = ((o_out, gq_out), (gk_out, gv_out))

    for more_x in range(n_inner):
        for more_z in range(2):
            @pl.when(jnp.logical_and(inner == more_x, first == (more_z == 0)))
            def _(more=more_x + more_z):
                pl.semaphore_wait(barrier, peers - 1 + more)

    def scatter(phase, recv):
        def chunk(c, carry):
            def one(p, carry):
                other, device = place(p)
                for a in range(2):
                    pltpu.make_async_remote_copy(
                        src_ref=sources[phase][a].at[:, column(other, c)],
                        dst_ref=xin.at[2 * phase + a, strip(me), cols(c)],
                        send_sem=in_send,
                        recv_sem=recv.at[c],
                        device_id=device,
                        device_id_type=MESH,
                    ).start()
                return carry

            lax.fori_loop(1, peers, one, 0)
            for a in range(2):
                pltpu.make_async_copy(
                    sources[phase][a].at[:, column(me, c)],
                    xin.at[2 * phase + a, strip(me), cols(c)],
                    recv.at[c],
                ).start()
            return carry

        lax.fori_loop(0, chunks, chunk, 0)

    scatter(0, first_recv)

    def rest(second_recv, chain_recv, t_recv, g_recv, out_send, out_recv,
             p_send, s_send, t_send, g_send, gain_sem, hop_send, hop_recv, own_sem, hold_sem,
             tail_send, tail_recv):
        in_recv = first_recv, second_recv

        def announce(p, carry):
            _, device = place(p)
            pl.semaphore_signal(entered.at[0], inc=1, device_id=device, device_id_type=MESH)
            return carry

        lax.fori_loop(1, peers, announce, 0)
        gains = pltpu.make_async_copy(gain_hbm, gain, gain_sem)
        gains.start()

        if n_inner == 2:
            @pl.when(jnp.logical_not(inside))
            def _():
                pl.semaphore_signal(entered.at[0], inc=1, device_id=across, device_id_type=MESH)

        @pl.when(jnp.logical_not(first))
        def _():
            pl.semaphore_signal(entered.at[0], inc=1, device_id=earlier, device_id_type=MESH)

        @pl.when(first)
        def _():
            def carried_in(c, carry):
                pltpu.make_async_copy(
                    s0_hbm.at[pl.ds(j * heads + c * step, step)], pin.at[piece(c)], chain_recv.at[c],
                ).start()
                return carry

            lax.fori_loop(0, chunks, carried_in, 0)

        @pl.when(last)
        def _():
            sin[...] = jnp.zeros_like(sin)

        row = lax.broadcasted_iota(jnp.int32, (block, block), 0)
        col = lax.broadcasted_iota(jnp.int32, (block, block), 1)
        causal = col <= row
        gains.wait()

        for more_x in range(n_inner):
            for more_z in range(2):
                @pl.when(jnp.logical_and(inner == n_inner - 1 - more_x, last == (more_z == 0)))
                def _(more=more_x + more_z):
                    pl.semaphore_wait(entered.at[0], peers - 1 + more)

        if n_inner == 2:
            @pl.when(inside)
            def _():
                pl.semaphore_signal(entered.at[1], inc=1, device_id=across, device_id_type=MESH)

        @pl.when(jnp.logical_not(last))
        def _():
            pl.semaphore_signal(entered.at[1], inc=1, device_id=later, device_id_type=MESH)

        if detours:
            @pl.when(owes)
            def _():
                pl.semaphore_signal(entered.at[2], inc=1, device_id=partner, device_id_type=MESH)

        scatter(1, second_recv)

        for more_x in range(n_inner):
            for more_z in range(2):
                if more_x + more_z > 0:
                    @pl.when(jnp.logical_and(inner == more_x, first == (more_z == 0)))
                    def _(more=more_x + more_z):
                        pl.semaphore_wait(entered.at[1], more)

        if detours:
            @pl.when(owes)
            def _():
                pl.semaphore_wait(entered.at[2], 1)

        def arrived(phase, c):
            ref = xin.at[pl.ds(2 * phase, 2), :, cols(c)]
            pltpu.make_async_copy(ref, ref, in_recv[phase].at[c]).wait()

        def give(phase, c):
            def back(p, carry):
                other, device = place(p)
                for a in range(2):
                    def send(dst, device, recv, a=a):
                        pltpu.make_async_remote_copy(
                            src_ref=xout.at[2 * phase + a, strip(other), cols(c)], dst_ref=dst,
                            send_sem=out_send, recv_sem=recv, device_id=device, device_id_type=MESH,
                        ).start()

                    target = targets[phase][a].at[:, column(me, c)]
                    if detours and phase == 0 and a < DETOUR_ARRAYS:
                        detour = jnp.logical_and(owes, jnp.logical_and(c < DETOUR_CHUNKS, p == 1))

                        @pl.when(detour)
                        def _():
                            send(hop.at[a, :, cols(c)], hop_device, hop_recv)

                        @pl.when(jnp.logical_not(detour))
                        def _():
                            send(target, device, out_recv)
                    elif late and phase == 1:
                        held = jnp.logical_and(p == 1, c >= chunks - late)

                        @pl.when(held)
                        def _(a=a):
                            at = pl.multiple_of((c - (chunks - late)) * span, span)
                            pltpu.make_async_copy(
                                xout.at[2 + a, strip(other), cols(c)],
                                hold.at[a, :, pl.ds(at, span)], hold_sem).start()

                        @pl.when(jnp.logical_not(held))
                        def _():
                            send(target, device, out_recv)
                    else:
                        send(target, device, out_recv)
                return carry

            lax.fori_loop(1, peers, back, 0)
            for a in range(2):
                pltpu.make_async_copy(
                    xout.at[2 * phase + a, strip(me), cols(c)],
                    targets[phase][a].at[:, column(me, c)],
                    own_sem,
                ).start()

        def state_copy(src, dst, send, recv, c, device):
            return pltpu.make_async_remote_copy(
                src_ref=src.at[piece(c)], dst_ref=dst.at[piece(c)], send_sem=send,
                recv_sem=recv.at[c], device_id=device, device_id_type=MESH)

        def landed(ref, recv, c):
            pltpu.make_async_copy(ref.at[piece(c)], ref.at[piece(c)], recv.at[c]).wait()

        def lanes(c, h):
            return pl.ds(pl.multiple_of(c * span + h * HEAD_DIM, HEAD_DIM), HEAD_DIM)

        def block_states(c):
            arrived(0, c)
            for h in range(step):
                n, hc = c * step + h, lanes(c, h)
                run = dot(xin[0, :block, hc], xin[1, :block, hc], TN)
                for b in range(1, sub):
                    r = slice(b * block, (b + 1) * block)
                    cum[n, b - 1] = run
                    run = run + dot(xin[0, r, hc], xin[1, r, hc], TN)
                tot[n] = run
            if n_inner == 2:
                state_copy(tot, xt, t_send, t_recv, c, across).start()

        def pass_prefix(c):
            if n_inner == 2:
                landed(xt, t_recv, c)
            landed(pin, chain_recv, c)

            @pl.when(jnp.logical_not(last))
            def _():
                for h in range(step):
                    n = c * step + h
                    psend[n] = pin[n] + tot[n] + xt[n] if n_inner == 2 else pin[n] + tot[n]
                state_copy(psend, pin, p_send, chain_recv, c, later).start()

            for h in range(step):
                n = c * step + h
                before = pin[n]
                if n_inner == 2:
                    before = before + jnp.where(inner == 1, xt[n], 0.0)
                prefix[n, 0] = before.astype(BF16)
                for b in range(1, sub):
                    prefix[n, b] = (before + cum[n, b - 1]).astype(BF16)

        def attend(c):
            arrived(1, c)
            for h in range(step):
                n, hc = c * step + h, lanes(c, h)
                at = pl.multiple_of((j * heads + n) * HEAD_DIM, HEAD_DIM)
                g = gain[pl.ds(at, HEAD_DIM)].reshape(1, HEAD_DIM)
                run = None
                for b in reversed(range(sub)):
                    r = slice(b * block, (b + 1) * block)
                    k, v, q, up = xin[0, r, hc], xin[1, r, hc], xin[2, r, hc], xin[3, r, hc]
                    state = prefix[n, b]
                    w = jnp.where(causal, dot(q, k, NT), 0.0).astype(BF16)
                    att = dot(w, v, NN) + dot(q, state, NN)
                    inv = lax.rsqrt(jnp.mean(att * att, axis=-1, keepdims=True) + EPSILON)
                    normed = att * inv
                    xout[0, r, hc] = (normed * g).astype(BF16)
                    scaled = up.astype(F32) * g
                    ga = ((scaled - normed * jnp.mean(scaled * normed, axis=-1, keepdims=True))
                          * inv).astype(BF16)
                    gw = jnp.where(causal, dot(ga, v, NT), 0.0).astype(BF16)
                    xout[1, r, hc] = (dot(gw, k, NN) + dot(ga, state, NT)).astype(BF16)
                    part[0, r, hc] = dot(gw, q, TN)
                    part[1, r, hc] = dot(w, ga, TN)
                    if run is not None:
                        gcum[n, b] = run
                    grad = dot(q, ga, TN)
                    run = grad if run is None else run + grad
                gtot[n] = run
            if n_inner == 2:
                state_copy(gtot, xg, g_send, g_recv, c, across).start()
            give(0, c)

        def finish(c):
            if n_inner == 2:
                landed(xg, g_recv, c)

            @pl.when(jnp.logical_not(last))
            def _():
                landed(sin, chain_recv, c)

            @pl.when(jnp.logical_not(first))
            def _():
                for h in range(step):
                    n = c * step + h
                    ssend[n] = sin[n] + gtot[n] + xg[n] if n_inner == 2 else sin[n] + gtot[n]
                state_copy(ssend, sin, s_send, chain_recv, c, earlier).start()

            for h in range(step):
                n, hc = c * step + h, lanes(c, h)
                after = sin[n]
                if n_inner == 2:
                    after = after + jnp.where(inner == 0, xg[n], 0.0)
                for b in range(sub):
                    r = slice(b * block, (b + 1) * block)
                    suffix = (after + gcum[n, b] if b < sub - 1 else after).astype(BF16)
                    xout[2, r, hc] = (part[0, r, hc] + dot(xin[1, r, hc], suffix, NT)).astype(BF16)
                    xout[3, r, hc] = (part[1, r, hc] + dot(xin[0, r, hc], suffix, NN)).astype(BF16)
            give(1, c)

        prefix_lag = jnp.minimum(2 + 2 * outer, chunks)
        suffix_lag = chunks + 2 + 2 * (n_outer - 1 - outer)

        def tick(i, carry):
            @pl.when(i < chunks)
            def _():
                block_states(i)

            @pl.when(jnp.logical_and(i >= prefix_lag, i < prefix_lag + chunks))
            def _():
                pass_prefix(i - prefix_lag)

            @pl.when(jnp.logical_and(i >= chunks, i < 2 * chunks))
            def _():
                attend(i - chunks)

            @pl.when(jnp.logical_and(i >= suffix_lag, i < suffix_lag + chunks))
            def _():
                finish(i - suffix_lag)

            return carry

        lax.fori_loop(0, 2 * chunks + 2 * n_outer, tick, 0)

        if detours:
            @pl.when(relays)
            def _():
                pltpu.make_async_copy(hop, hop, hop_recv).wait()
                first_head = (1 - hd) * (sub * heads) + j * heads
                whole = pl.ds(pl.multiple_of(first_head * HEAD_DIM, span), hop.shape[2])
                for a in range(DETOUR_ARRAYS):
                    pltpu.make_async_remote_copy(
                        src_ref=hop.at[a], dst_ref=targets[0][a].at[:, whole], send_sem=hop_send,
                        recv_sem=out_recv, device_id=passed_to, device_id_type=MESH).start()
                pltpu.make_async_copy(hop, hop, hop_send).wait()

        sent = xin.at[:, pl.ds(0, (peers - 1) * rows)]
        back = xin.at[:, :, pl.ds(0, 5 * chunks // 8 * span)] if late else sent
        mine = xin.at[:, pl.ds(0, rows)]
        if late:
            to_partner = pltpu.make_async_remote_copy(
                src_ref=hold, dst_ref=tail, send_sem=tail_send, recv_sem=tail_recv,
                device_id=partner, device_id_type=MESH)
            pltpu.make_async_copy(hold, hold, hold_sem).wait()

            @pl.when(j == sub - 1)
            def _():
                to_partner.start()

        pltpu.make_async_copy(sent, sent, in_send).wait()
        pltpu.make_async_copy(back, back, out_send).wait()
        pltpu.make_async_copy(mine, mine, own_sem).wait()
        if n_inner == 2:
            pltpu.make_async_copy(tot, tot, t_send).wait()
            pltpu.make_async_copy(gtot, gtot, g_send).wait()

        @pl.when(jnp.logical_not(last))
        def _():
            pltpu.make_async_copy(psend, psend, p_send).wait()

        @pl.when(jnp.logical_not(first))
        def _():
            pltpu.make_async_copy(ssend, ssend, s_send).wait()

        pltpu.make_async_copy(back, back, out_recv).wait()
        if late:
            @pl.when(j == sub - 1)
            def _():
                to_partner.wait()

    one = pltpu.SemaphoreType.DMA
    chain = one((chunks,))
    pl.run_scoped(rest, chain, chain, chain, chain, *[one] * 13)


def land(*refs):
    sources, targets, sem = refs[:4], refs[-5:-1], refs[-1]
    copies = [pltpu.make_async_copy(src, dst, sem) for src, dst in zip(sources, targets)]
    for copy in copies:
        copy.start()
    for copy in copies:
        copy.wait()


def last_pieces(sub, hold, tail, written, out, sem, send, recv):
    seq, hd = lax.axis_index("seq"), lax.axis_index("head")
    partner = (seq, 1 - hd)
    barrier = pltpu.get_barrier_semaphore()

    @pl.when(lax.rem(seq, sub) < sub - 1)
    def _():
        pl.semaphore_signal(barrier, inc=1, device_id=partner, device_id_type=MESH)
        pl.semaphore_wait(barrier, 1)
        copy = pltpu.make_async_remote_copy(
            src_ref=hold, dst_ref=out, send_sem=send, recv_sem=recv,
            device_id=partner, device_id_type=MESH)
        copy.start()
        copy.wait()

    @pl.when(lax.rem(seq, sub) == sub - 1)
    def _():
        copy = pltpu.make_async_copy(tail, out, sem)
        copy.start()
        copy.wait()


def land_last(plan, tail, gk_in, gv_in, gk_out, gv_out, sem):
    n_outer, n_inner, sub, n_head, rows, heads, step, late = plan
    seq, hd = lax.axis_index("seq"), lax.axis_index("head")
    first = (1 - hd) * (sub * heads) + lax.rem(seq, sub) * heads + heads - late * step
    at = pl.ds(pl.multiple_of(first * HEAD_DIM, HEAD_DIM), late * step * HEAD_DIM)
    copies = [pltpu.make_async_copy(tail.at[a], out.at[:, at], sem)
              for a, out in enumerate((gk_out, gv_out))]
    for copy in copies:
        copy.start()
    for copy in copies:
        copy.wait()


def per_device(mesh, query, key, value, cotangent, gain, incoming_state):
    n_seq, n_head = mesh.shape["seq"], mesh.shape["head"]
    rows, features = query.shape
    local_heads = incoming_state.shape[0]
    sub = 2 if n_seq % 2 == 0 and local_heads % 2 == 0 else 1
    n_inner = 2 if n_seq % (2 * sub) == 0 else 1
    n_outer = n_seq // (sub * n_inner)
    heads = local_heads // sub
    step = next(s for s in range(max(1, heads // 8), heads + 1) if heads % s == 0)
    chunks = heads // step
    tokens = rows * n_head * sub
    width = heads * HEAD_DIM
    splits = sub == 2 and n_head == 2 and n_inner == 2 and n_outer > 1 and chunks % 8 == 0
    late = chunks if splits else 0
    plan = (n_outer, n_inner, sub, n_head, rows, heads, step, late)
    anywhere = pl.BlockSpec(memory_space=pl.ANY)
    resident = pl.BlockSpec(memory_space=pltpu.HBM)
    state = pltpu.VMEM((heads, HEAD_DIM, HEAD_DIM), F32)
    states = pltpu.VMEM((heads, max(1, sub - 1), HEAD_DIM, HEAD_DIM), F32)
    shapes = [jax.ShapeDtypeStruct((rows, features), BF16)] * 4
    pieces = [jax.ShapeDtypeStruct((2, rows, max(1, late) * step * HEAD_DIM), BF16)] * 2
    *results, hold, tail = pl.pallas_call(
        functools.partial(kernel, plan),
        out_shape=shapes + pieces,
        in_specs=[resident] * 6,
        out_specs=[anywhere] * 6,
        scratch_shapes=[
            pltpu.VMEM((4, tokens, width), BF16),
            pltpu.VMEM((4, tokens, width), BF16),
            pltpu.VMEM((2, tokens, width), F32),
            states, states,
            pltpu.VMEM((heads, sub, HEAD_DIM, HEAD_DIM), BF16),
            state, state, state, state, state, state, state, state,
            pltpu.VMEM((local_heads * HEAD_DIM,), F32),
            pltpu.VMEM((DETOUR_ARRAYS, rows, DETOUR_CHUNKS * step * HEAD_DIM), BF16),
            pltpu.SemaphoreType.DMA((chunks,)), pltpu.SemaphoreType.DMA,
            pltpu.SemaphoreType.REGULAR((3,)),
        ],
        compiler_params=pltpu.CompilerParams(
            collective_id=0, has_side_effects=True, vmem_limit_bytes=VMEM),
    )(*(pltpu.with_memory_space_constraint(x, pltpu.HBM)
        for x in (query, key, value, cotangent, gain, incoming_state)))
    small = pltpu.CompilerParams(vmem_limit_bytes=1024 * 1024)
    written = pl.pallas_call(
        land,
        out_shape=shapes,
        in_specs=[anywhere] * 4,
        out_specs=[anywhere] * 4,
        scratch_shapes=[pltpu.SemaphoreType.DMA],
        compiler_params=small,
    )(*results)
    if not late:
        return tuple(written)
    output, grad_query, grad_key, grad_value = written
    tail = pl.pallas_call(
        functools.partial(last_pieces, sub),
        out_shape=pieces[0],
        in_specs=[anywhere] * 3,
        out_specs=anywhere,
        scratch_shapes=[pltpu.SemaphoreType.DMA] * 3,
        compiler_params=pltpu.CompilerParams(
            collective_id=1, has_side_effects=True, vmem_limit_bytes=1024 * 1024),
    )(hold, tail, pltpu.with_memory_space_constraint(grad_key, pltpu.HBM))
    grad_key, grad_value = pl.pallas_call(
        functools.partial(land_last, plan),
        out_shape=shapes[:2],
        in_specs=[anywhere] * 3,
        out_specs=[anywhere] * 2,
        input_output_aliases={1: 0, 2: 1},
        scratch_shapes=[pltpu.SemaphoreType.DMA],
        compiler_params=small,
    )(tail, grad_key, grad_value)
    return output, grad_query, grad_key, grad_value


def solution(mesh):
    tokens = P(("seq", "head"), None)
    return jax.shard_map(
        functools.partial(per_device, mesh),
        mesh=mesh,
        in_specs=(tokens, tokens, tokens, tokens, P("head"), P("head", None, None)),
        out_specs=(tokens, tokens, tokens, tokens),
        check_vma=False,
    )
```

```python
import functools

import jax
import jax.numpy as jnp
from jax import lax
from jax.experimental import pallas as pl
from jax.experimental.pallas import tpu as pltpu
from jax.sharding import PartitionSpec as P

HEAD_DIM = 128
EPSILON = 1e-06
VMEM = 36000 * 1024
DETOUR_ARRAYS, DETOUR_CHUNKS = 1, 1
MESH = pl.DeviceIdType.MESH
F32 = jnp.float32
BF16 = jnp.bfloat16

NT = (((1,), (1,)), ((), ()))
TN = (((0,), (0,)), ((), ()))
NN = (((1,), (0,)), ((), ()))


def dot(a, b, dims):
    return lax.dot_general(a, b, dims, preferred_element_type=F32)


def kernel(plan, q_hbm, k_hbm, v_hbm, y_hbm, gain_hbm, s0_hbm, o_out, gq_out, gk_out, gv_out,
           hold, tail, xin, xout, part, cum, gcum, prefix, tot, gtot, xt, xg, pin, psend, sin, ssend, gain, hop,
           stage, first_recv, in_send, stage_sem, entered):
    n_outer, n_inner, sub, n_head, rows, heads, step, late = plan
    peers = sub * n_head
    chunks = heads // step
    block = rows * n_head
    span = step * HEAD_DIM
    seq, hd = lax.axis_index("seq"), lax.axis_index("head")
    group, j = seq // sub, lax.rem(seq, sub)
    outer, inner = group // n_inner, lax.rem(group, n_inner)
    me = j * n_head + hd

    def place(p):
        to_j = lax.rem(j + p // n_head, sub)
        to_hd = lax.rem(hd + lax.rem(p, n_head), n_head)
        return to_j * n_head + to_hd, (group * sub + to_j, to_hd)

    def column(other, c):
        owner = lax.rem(other, n_head) * (sub * heads) + (other // n_head) * heads + c * step
        return pl.ds(pl.multiple_of(owner * HEAD_DIM, span), span)

    def strip(index):
        return pl.ds(pl.multiple_of(index * rows, rows), rows)

    def cols(c):
        return pl.ds(pl.multiple_of(c * span, span), span)

    def piece(c):
        return pl.ds(c * step, step)

    across = ((outer * n_inner + (n_inner - 1 - inner)) * sub + j, hd)
    later = (seq + n_inner * sub, hd)
    earlier = (seq - n_inner * sub, hd)
    first, last = outer == 0, outer == n_outer - 1
    detours = n_outer > 1 and n_inner == 2 and n_head == 2
    partner = (seq, n_head - 1 - hd)
    by_x = j == 0
    hop_device = (jnp.where(by_x, across[0], later[0]), n_head - 1 - hd)
    owes = group == 0
    relays = group == jnp.where(by_x, 1, n_inner)
    passed_to = (jnp.where(by_x, across[0], earlier[0]), hd)
    barrier = pltpu.get_barrier_semaphore()

    def greet(p, carry):
        _, device = place(p)
        pl.semaphore_signal(barrier, inc=1, device_id=device, device_id_type=MESH)
        return carry

    lax.fori_loop(1, peers, greet, 0)
    inside = inner == 0

    if n_inner == 2:
        @pl.when(inside)
        def _():
            pl.semaphore_signal(barrier, inc=1, device_id=across, device_id_type=MESH)

    @pl.when(jnp.logical_not(last))
    def _():
        pl.semaphore_signal(barrier, inc=1, device_id=later, device_id_type=MESH)

    sources = ((k_hbm, v_hbm), (q_hbm, y_hbm))
    targets = ((o_out, gq_out), (gk_out, gv_out))

    early = hd == 0
    beside, beside_device = place(1)
    staging = [
        pltpu.make_async_copy(sources[0][a].at[:, column(beside, 0)], stage.at[a], stage_sem)
        for a in range(2)
    ]

    @pl.when(early)
    def _():
        for copy in staging:
            copy.start()

    for more_x in range(n_inner):
        for more_z in range(2):
            @pl.when(jnp.logical_and(inner == more_x, first == (more_z == 0)))
            def _(more=more_x + more_z):
                pl.semaphore_wait(barrier, peers - 1 + more)

    def scatter(phase, recv, staged):
        def chunk(c, carry):
            def one(p, carry):
                other, device = place(p)
                for a in range(2):
                    pltpu.make_async_remote_copy(
                        src_ref=sources[phase][a].at[:, column(other, c)],
                        dst_ref=xin.at[2 * phase + a, strip(me), cols(c)],
                        send_sem=in_send,
                        recv_sem=recv.at[c],
                        device_id=device,
                        device_id_type=MESH,
                    ).start()
                return carry

            lax.fori_loop(jnp.where(c < staged, 2, 1), peers, one, 0)
            for a in range(2):
                pltpu.make_async_copy(
                    sources[phase][a].at[:, column(me, c)],
                    xin.at[2 * phase + a, strip(me), cols(c)],
                    recv.at[c],
                ).start()
            return carry

        lax.fori_loop(0, chunks, chunk, 0)

    @pl.when(early)
    def _():
        pltpu.make_async_copy(stage, stage, stage_sem).wait()
        for a in range(2):
            pltpu.make_async_remote_copy(
                src_ref=stage.at[a],
                dst_ref=xin.at[a, strip(me), cols(0)],
                send_sem=in_send,
                recv_sem=first_recv.at[0],
                device_id=beside_device,
                device_id_type=MESH,
            ).start()

    scatter(0, first_recv, jnp.where(early, 1, 0))

    def rest(second_recv, chain_recv, t_recv, g_recv, out_send, out_recv,
             p_send, s_send, t_send, g_send, gain_sem, hop_send, hop_recv, own_sem, hold_sem,
             tail_send, tail_recv):
        in_recv = first_recv, second_recv

        def announce(p, carry):
            _, device = place(p)
            pl.semaphore_signal(entered.at[0], inc=1, device_id=device, device_id_type=MESH)
            return carry

        lax.fori_loop(1, peers, announce, 0)
        gains = pltpu.make_async_copy(gain_hbm, gain, gain_sem)
        gains.start()

        if n_inner == 2:
            @pl.when(jnp.logical_not(inside))
            def _():
                pl.semaphore_signal(entered.at[0], inc=1, device_id=across, device_id_type=MESH)

        @pl.when(jnp.logical_not(first))
        def _():
            pl.semaphore_signal(entered.at[0], inc=1, device_id=earlier, device_id_type=MESH)

        @pl.when(first)
        def _():
            def carried_in(c, carry):
                pltpu.make_async_copy(
                    s0_hbm.at[pl.ds(j * heads + c * step, step)], pin.at[piece(c)], chain_recv.at[c],
                ).start()
                return carry

            lax.fori_loop(0, chunks, carried_in, 0)

        @pl.when(last)
        def _():
            sin[...] = jnp.zeros_like(sin)

        row = lax.broadcasted_iota(jnp.int32, (block, block), 0)
        col = lax.broadcasted_iota(jnp.int32, (block, block), 1)
        causal = col <= row
        gains.wait()

        for more_x in range(n_inner):
            for more_z in range(2):
                @pl.when(jnp.logical_and(inner == n_inner - 1 - more_x, last == (more_z == 0)))
                def _(more=more_x + more_z):
                    pl.semaphore_wait(entered.at[0], peers - 1 + more)

        if n_inner == 2:
            @pl.when(inside)
            def _():
                pl.semaphore_signal(entered.at[1], inc=1, device_id=across, device_id_type=MESH)

        @pl.when(jnp.logical_not(last))
        def _():
            pl.semaphore_signal(entered.at[1], inc=1, device_id=later, device_id_type=MESH)

        if detours:
            @pl.when(owes)
            def _():
                pl.semaphore_signal(entered.at[2], inc=1, device_id=partner, device_id_type=MESH)

        scatter(1, second_recv, 0)

        for more_x in range(n_inner):
            for more_z in range(2):
                if more_x + more_z > 0:
                    @pl.when(jnp.logical_and(inner == more_x, first == (more_z == 0)))
                    def _(more=more_x + more_z):
                        pl.semaphore_wait(entered.at[1], more)

        if detours:
            @pl.when(owes)
            def _():
                pl.semaphore_wait(entered.at[2], 1)

        def arrived(phase, c):
            ref = xin.at[pl.ds(2 * phase, 2), :, cols(c)]
            pltpu.make_async_copy(ref, ref, in_recv[phase].at[c]).wait()

        def give(phase, c):
            def back(p, carry):
                other, device = place(p)
                for a in range(2):
                    def send(dst, device, recv, a=a):
                        pltpu.make_async_remote_copy(
                            src_ref=xout.at[2 * phase + a, strip(other), cols(c)], dst_ref=dst,
                            send_sem=out_send, recv_sem=recv, device_id=device, device_id_type=MESH,
                        ).start()

                    target = targets[phase][a].at[:, column(me, c)]
                    if detours and phase == 0 and a < DETOUR_ARRAYS:
                        detour = jnp.logical_and(owes, jnp.logical_and(c < DETOUR_CHUNKS, p == 1))

                        @pl.when(detour)
                        def _():
                            send(hop.at[a, :, cols(c)], hop_device, hop_recv)

                        @pl.when(jnp.logical_not(detour))
                        def _():
                            send(target, device, out_recv)
                    elif late and phase == 1:
                        held = jnp.logical_and(p == 1, c >= chunks - late)

                        @pl.when(held)
                        def _(a=a):
                            at = pl.multiple_of((c - (chunks - late)) * span, span)
                            pltpu.make_async_copy(
                                xout.at[2 + a, strip(other), cols(c)],
                                hold.at[a, :, pl.ds(at, span)], hold_sem).start()

                        @pl.when(jnp.logical_not(held))
                        def _():
                            send(target, device, out_recv)
                    else:
                        send(target, device, out_recv)
                return carry

            lax.fori_loop(1, peers, back, 0)
            for a in range(2):
                pltpu.make_async_copy(
                    xout.at[2 * phase + a, strip(me), cols(c)],
                    targets[phase][a].at[:, column(me, c)],
                    own_sem,
                ).start()

        def state_copy(src, dst, send, recv, c, device):
            return pltpu.make_async_remote_copy(
                src_ref=src.at[piece(c)], dst_ref=dst.at[piece(c)], send_sem=send,
                recv_sem=recv.at[c], device_id=device, device_id_type=MESH)

        def landed(ref, recv, c):
            pltpu.make_async_copy(ref.at[piece(c)], ref.at[piece(c)], recv.at[c]).wait()

        def lanes(c, h):
            return pl.ds(pl.multiple_of(c * span + h * HEAD_DIM, HEAD_DIM), HEAD_DIM)

        def block_states(c):
            arrived(0, c)
            for h in range(step):
                n, hc = c * step + h, lanes(c, h)
                run = dot(xin[0, :block, hc], xin[1, :block, hc], TN)
                for b in range(1, sub):
                    r = slice(b * block, (b + 1) * block)
                    cum[n, b - 1] = run
                    run = run + dot(xin[0, r, hc], xin[1, r, hc], TN)
                tot[n] = run
            if n_inner == 2:
                state_copy(tot, xt, t_send, t_recv, c, across).start()

        def pass_prefix(c):
            if n_inner == 2:
                landed(xt, t_recv, c)
            landed(pin, chain_recv, c)

            @pl.when(jnp.logical_not(last))
            def _():
                for h in range(step):
                    n = c * step + h
                    psend[n] = pin[n] + tot[n] + xt[n] if n_inner == 2 else pin[n] + tot[n]
                state_copy(psend, pin, p_send, chain_recv, c, later).start()

            for h in range(step):
                n = c * step + h
                before = pin[n]
                if n_inner == 2:
                    before = before + jnp.where(inner == 1, xt[n], 0.0)
                prefix[n, 0] = before.astype(BF16)
                for b in range(1, sub):
                    prefix[n, b] = (before + cum[n, b - 1]).astype(BF16)

        def attend(c):
            arrived(1, c)
            for h in range(step):
                n, hc = c * step + h, lanes(c, h)
                at = pl.multiple_of((j * heads + n) * HEAD_DIM, HEAD_DIM)
                g = gain[pl.ds(at, HEAD_DIM)].reshape(1, HEAD_DIM)
                run = None
                for b in reversed(range(sub)):
                    r = slice(b * block, (b + 1) * block)
                    k, v, q, up = xin[0, r, hc], xin[1, r, hc], xin[2, r, hc], xin[3, r, hc]
                    state = prefix[n, b]
                    w = jnp.where(causal, dot(q, k, NT), 0.0).astype(BF16)
                    att = dot(w, v, NN) + dot(q, state, NN)
                    inv = lax.rsqrt(jnp.mean(att * att, axis=-1, keepdims=True) + EPSILON)
                    normed = att * inv
                    xout[0, r, hc] = (normed * g).astype(BF16)
                    scaled = up.astype(F32) * g
                    ga = ((scaled - normed * jnp.mean(scaled * normed, axis=-1, keepdims=True))
                          * inv).astype(BF16)
                    gw = jnp.where(causal, dot(ga, v, NT), 0.0).astype(BF16)
                    xout[1, r, hc] = (dot(gw, k, NN) + dot(ga, state, NT)).astype(BF16)
                    part[0, r, hc] = dot(gw, q, TN)
                    part[1, r, hc] = dot(w, ga, TN)
                    if run is not None:
                        gcum[n, b] = run
                    grad = dot(q, ga, TN)
                    run = grad if run is None else run + grad
                gtot[n] = run
            if n_inner == 2:
                state_copy(gtot, xg, g_send, g_recv, c, across).start()
            give(0, c)

        def finish(c):
            if n_inner == 2:
                landed(xg, g_recv, c)

            @pl.when(jnp.logical_not(last))
            def _():
                landed(sin, chain_recv, c)

            @pl.when(jnp.logical_not(first))
            def _():
                for h in range(step):
                    n = c * step + h
                    ssend[n] = sin[n] + gtot[n] + xg[n] if n_inner == 2 else sin[n] + gtot[n]
                state_copy(ssend, sin, s_send, chain_recv, c, earlier).start()

            for h in range(step):
                n, hc = c * step + h, lanes(c, h)
                after = sin[n]
                if n_inner == 2:
                    after = after + jnp.where(inner == 0, xg[n], 0.0)
                for b in range(sub):
                    r = slice(b * block, (b + 1) * block)
                    suffix = (after + gcum[n, b] if b < sub - 1 else after).astype(BF16)
                    xout[2, r, hc] = (part[0, r, hc] + dot(xin[1, r, hc], suffix, NT)).astype(BF16)
                    xout[3, r, hc] = (part[1, r, hc] + dot(xin[0, r, hc], suffix, NN)).astype(BF16)
            give(1, c)

        prefix_lag = jnp.minimum(2 + 2 * outer, chunks)
        suffix_lag = chunks + 2 + 2 * (n_outer - 1 - outer)

        def tick(i, carry):
            @pl.when(i < chunks)
            def _():
                block_states(i)

            @pl.when(jnp.logical_and(i >= prefix_lag, i < prefix_lag + chunks))
            def _():
                pass_prefix(i - prefix_lag)

            @pl.when(jnp.logical_and(i >= chunks, i < 2 * chunks))
            def _():
                attend(i - chunks)

            @pl.when(jnp.logical_and(i >= suffix_lag, i < suffix_lag + chunks))
            def _():
                finish(i - suffix_lag)

            return carry

        lax.fori_loop(0, 2 * chunks + 2 * n_outer, tick, 0)

        if detours:
            @pl.when(relays)
            def _():
                pltpu.make_async_copy(hop, hop, hop_recv).wait()
                first_head = (1 - hd) * (sub * heads) + j * heads
                whole = pl.ds(pl.multiple_of(first_head * HEAD_DIM, span), hop.shape[2])
                for a in range(DETOUR_ARRAYS):
                    pltpu.make_async_remote_copy(
                        src_ref=hop.at[a], dst_ref=targets[0][a].at[:, whole], send_sem=hop_send,
                        recv_sem=out_recv, device_id=passed_to, device_id_type=MESH).start()
                pltpu.make_async_copy(hop, hop, hop_send).wait()

        sent = xin.at[:, pl.ds(0, (peers - 1) * rows)]
        back = xin.at[:, :, pl.ds(0, 5 * chunks // 8 * span)] if late else sent
        mine = xin.at[:, pl.ds(0, rows)]
        if late:
            to_partner = pltpu.make_async_remote_copy(
                src_ref=hold, dst_ref=tail, send_sem=tail_send, recv_sem=tail_recv,
                device_id=partner, device_id_type=MESH)
            pltpu.make_async_copy(hold, hold, hold_sem).wait()

            @pl.when(j == sub - 1)
            def _():
                to_partner.start()

        pltpu.make_async_copy(sent, sent, in_send).wait()
        pltpu.make_async_copy(back, back, out_send).wait()
        pltpu.make_async_copy(mine, mine, own_sem).wait()
        if n_inner == 2:
            pltpu.make_async_copy(tot, tot, t_send).wait()
            pltpu.make_async_copy(gtot, gtot, g_send).wait()

        @pl.when(jnp.logical_not(last))
        def _():
            pltpu.make_async_copy(psend, psend, p_send).wait()

        @pl.when(jnp.logical_not(first))
        def _():
            pltpu.make_async_copy(ssend, ssend, s_send).wait()

        pltpu.make_async_copy(back, back, out_recv).wait()
        if late:
            @pl.when(j == sub - 1)
            def _():
                to_partner.wait()

    one = pltpu.SemaphoreType.DMA
    chain = one((chunks,))
    pl.run_scoped(rest, chain, chain, chain, chain, *[one] * 13)


def land(*refs):
    sources, targets, sem = refs[:4], refs[-5:-1], refs[-1]
    copies = [pltpu.make_async_copy(src, dst, sem) for src, dst in zip(sources, targets)]
    for copy in copies:
        copy.start()
    for copy in copies:
        copy.wait()


def last_pieces(sub, hold, tail, written, out, sem, send, recv):
    seq, hd = lax.axis_index("seq"), lax.axis_index("head")
    partner = (seq, 1 - hd)
    barrier = pltpu.get_barrier_semaphore()

    @pl.when(lax.rem(seq, sub) < sub - 1)
    def _():
        pl.semaphore_signal(barrier, inc=1, device_id=partner, device_id_type=MESH)
        pl.semaphore_wait(barrier, 1)
        copy = pltpu.make_async_remote_copy(
            src_ref=hold, dst_ref=out, send_sem=send, recv_sem=recv,
            device_id=partner, device_id_type=MESH)
        copy.start()
        copy.wait()

    @pl.when(lax.rem(seq, sub) == sub - 1)
    def _():
        copy = pltpu.make_async_copy(tail, out, sem)
        copy.start()
        copy.wait()


def land_last(plan, tail, gk_in, gv_in, gk_out, gv_out, sem):
    n_outer, n_inner, sub, n_head, rows, heads, step, late = plan
    seq, hd = lax.axis_index("seq"), lax.axis_index("head")
    first = (1 - hd) * (sub * heads) + lax.rem(seq, sub) * heads + heads - late * step
    at = pl.ds(pl.multiple_of(first * HEAD_DIM, HEAD_DIM), late * step * HEAD_DIM)
    copies = [pltpu.make_async_copy(tail.at[a], out.at[:, at], sem)
              for a, out in enumerate((gk_out, gv_out))]
    for copy in copies:
        copy.start()
    for copy in copies:
        copy.wait()


def per_device(mesh, query, key, value, cotangent, gain, incoming_state):
    n_seq, n_head = mesh.shape["seq"], mesh.shape["head"]
    rows, features = query.shape
    local_heads = incoming_state.shape[0]
    sub = 2 if n_seq % 2 == 0 and local_heads % 2 == 0 else 1
    n_inner = 2 if n_seq % (2 * sub) == 0 else 1
    n_outer = n_seq // (sub * n_inner)
    heads = local_heads // sub
    step = next(s for s in range(max(1, heads // 8), heads + 1) if heads % s == 0)
    chunks = heads // step
    tokens = rows * n_head * sub
    width = heads * HEAD_DIM
    splits = sub == 2 and n_head == 2 and n_inner == 2 and n_outer > 1 and chunks % 8 == 0
    late = chunks if splits else 0
    plan = (n_outer, n_inner, sub, n_head, rows, heads, step, late)
    anywhere = pl.BlockSpec(memory_space=pl.ANY)
    resident = pl.BlockSpec(memory_space=pltpu.HBM)
    state = pltpu.VMEM((heads, HEAD_DIM, HEAD_DIM), F32)
    states = pltpu.VMEM((heads, max(1, sub - 1), HEAD_DIM, HEAD_DIM), F32)
    shapes = [jax.ShapeDtypeStruct((rows, features), BF16)] * 4
    pieces = [jax.ShapeDtypeStruct((2, rows, max(1, late) * step * HEAD_DIM), BF16)] * 2
    *results, hold, tail = pl.pallas_call(
        functools.partial(kernel, plan),
        out_shape=shapes + pieces,
        in_specs=[resident] * 6,
        out_specs=[anywhere] * 6,
        scratch_shapes=[
            pltpu.VMEM((4, tokens, width), BF16),
            pltpu.VMEM((4, tokens, width), BF16),
            pltpu.VMEM((2, tokens, width), F32),
            states, states,
            pltpu.VMEM((heads, sub, HEAD_DIM, HEAD_DIM), BF16),
            state, state, state, state, state, state, state, state,
            pltpu.VMEM((local_heads * HEAD_DIM,), F32),
            pltpu.VMEM((DETOUR_ARRAYS, rows, DETOUR_CHUNKS * step * HEAD_DIM), BF16),
            pltpu.VMEM((2, rows, step * HEAD_DIM), BF16),
            pltpu.SemaphoreType.DMA((chunks,)), pltpu.SemaphoreType.DMA, pltpu.SemaphoreType.DMA,
            pltpu.SemaphoreType.REGULAR((3,)),
        ],
        compiler_params=pltpu.CompilerParams(
            collective_id=0, has_side_effects=True, vmem_limit_bytes=VMEM),
    )(*(pltpu.with_memory_space_constraint(x, pltpu.HBM)
        for x in (query, key, value, cotangent, gain, incoming_state)))
    small = pltpu.CompilerParams(vmem_limit_bytes=1024 * 1024)
    written = pl.pallas_call(
        land,
        out_shape=shapes,
        in_specs=[anywhere] * 4,
        out_specs=[anywhere] * 4,
        scratch_shapes=[pltpu.SemaphoreType.DMA],
        compiler_params=small,
    )(*results)
    if not late:
        return tuple(written)
    output, grad_query, grad_key, grad_value = written
    tail = pl.pallas_call(
        functools.partial(last_pieces, sub),
        out_shape=pieces[0],
        in_specs=[anywhere] * 3,
        out_specs=anywhere,
        scratch_shapes=[pltpu.SemaphoreType.DMA] * 3,
        compiler_params=pltpu.CompilerParams(
            collective_id=1, has_side_effects=True, vmem_limit_bytes=1024 * 1024),
    )(hold, tail, pltpu.with_memory_space_constraint(grad_key, pltpu.HBM))
    grad_key, grad_value = pl.pallas_call(
        functools.partial(land_last, plan),
        out_shape=shapes[:2],
        in_specs=[anywhere] * 3,
        out_specs=[anywhere] * 2,
        input_output_aliases={1: 0, 2: 1},
        scratch_shapes=[pltpu.SemaphoreType.DMA],
        compiler_params=small,
    )(tail, grad_key, grad_value)
    return output, grad_query, grad_key, grad_value


def solution(mesh):
    tokens = P(("seq", "head"), None)
    return jax.shard_map(
        functools.partial(per_device, mesh),
        mesh=mesh,
        in_specs=(tokens, tokens, tokens, tokens, P("head"), P("head", None, None)),
        out_specs=(tokens, tokens, tokens, tokens),
        check_vma=False,
    )
```

```python
import functools

import jax
import jax.numpy as jnp
from jax import lax
from jax.experimental import pallas as pl
from jax.experimental.pallas import tpu as pltpu
from jax.sharding import PartitionSpec as P

HEAD_DIM = 128
EPSILON = 1e-06
VMEM = 36000 * 1024
DETOUR_ARRAYS, DETOUR_CHUNKS = 1, 1
MESH = pl.DeviceIdType.MESH
F32 = jnp.float32
BF16 = jnp.bfloat16

NT = (((1,), (1,)), ((), ()))
TN = (((0,), (0,)), ((), ()))
NN = (((1,), (0,)), ((), ()))


def dot(a, b, dims):
    return lax.dot_general(a, b, dims, preferred_element_type=F32)


def kernel(plan, q_hbm, k_hbm, v_hbm, y_hbm, gain_hbm, s0_hbm, o_out, gq_out, gk_out, gv_out,
           hold, tail, xin, xout, part, cum, gcum, prefix, tot, gtot, xt, xg, pin, psend, sin, ssend, gain, hop,
           stage, first_recv, in_send, stage_sem, entered):
    n_outer, n_inner, sub, n_head, rows, heads, step, late = plan
    peers = sub * n_head
    chunks = heads // step
    block = rows * n_head
    span = step * HEAD_DIM
    seq, hd = lax.axis_index("seq"), lax.axis_index("head")
    group, j = seq // sub, lax.rem(seq, sub)
    outer, inner = group // n_inner, lax.rem(group, n_inner)
    me = j * n_head + hd

    def place(p):
        to_j = lax.rem(j + p // n_head, sub)
        to_hd = lax.rem(hd + lax.rem(p, n_head), n_head)
        return to_j * n_head + to_hd, (group * sub + to_j, to_hd)

    def column(other, c):
        owner = lax.rem(other, n_head) * (sub * heads) + (other // n_head) * heads + c * step
        return pl.ds(pl.multiple_of(owner * HEAD_DIM, span), span)

    def strip(index):
        return pl.ds(pl.multiple_of(index * rows, rows), rows)

    def cols(c):
        return pl.ds(pl.multiple_of(c * span, span), span)

    def piece(c):
        return pl.ds(c * step, step)

    across = ((outer * n_inner + (n_inner - 1 - inner)) * sub + j, hd)
    later = (seq + n_inner * sub, hd)
    earlier = (seq - n_inner * sub, hd)
    first, last = outer == 0, outer == n_outer - 1
    detours = n_outer > 1 and n_inner == 2 and n_head == 2
    partner = (seq, n_head - 1 - hd)
    by_x = j == 0
    hop_device = (jnp.where(by_x, across[0], later[0]), n_head - 1 - hd)
    owes = group == 0
    relays = group == jnp.where(by_x, 1, n_inner)
    passed_to = (jnp.where(by_x, across[0], earlier[0]), hd)
    barrier = pltpu.get_barrier_semaphore()

    def greet(p, carry):
        _, device = place(p)
        pl.semaphore_signal(barrier, inc=1, device_id=device, device_id_type=MESH)
        return carry

    lax.fori_loop(1, peers, greet, 0)
    inside = inner == 0

    if n_inner == 2:
        @pl.when(inside)
        def _():
            pl.semaphore_signal(barrier, inc=1, device_id=across, device_id_type=MESH)

    @pl.when(jnp.logical_not(last))
    def _():
        pl.semaphore_signal(barrier, inc=1, device_id=later, device_id_type=MESH)

    sources = ((k_hbm, v_hbm), (q_hbm, y_hbm))
    targets = ((o_out, gq_out), (gk_out, gv_out))

    early = hd == 0
    beside, beside_device = place(1)
    staging = [
        pltpu.make_async_copy(sources[0][a].at[:, column(beside, 0)], stage.at[a], stage_sem)
        for a in range(2)
    ]

    @pl.when(early)
    def _():
        for copy in staging:
            copy.start()

    for more_x in range(n_inner):
        for more_z in range(2):
            @pl.when(jnp.logical_and(inner == more_x, first == (more_z == 0)))
            def _(more=more_x + more_z):
                pl.semaphore_wait(barrier, peers - 1 + more)

    def scatter(phase, recv, staged):
        def chunk(c, carry):
            def one(q, carry):
                other, device = place(jnp.where(q == 1, 1, peers + 1 - q))
                for a in range(2):
                    pltpu.make_async_remote_copy(
                        src_ref=sources[phase][a].at[:, column(other, c)],
                        dst_ref=xin.at[2 * phase + a, strip(me), cols(c)],
                        send_sem=in_send,
                        recv_sem=recv.at[c],
                        device_id=device,
                        device_id_type=MESH,
                    ).start()
                return carry

            lax.fori_loop(jnp.where(c < staged, 2, 1), peers, one, 0)
            for a in range(2):
                pltpu.make_async_copy(
                    sources[phase][a].at[:, column(me, c)],
                    xin.at[2 * phase + a, strip(me), cols(c)],
                    recv.at[c],
                ).start()
            return carry

        lax.fori_loop(0, chunks, chunk, 0)

    @pl.when(early)
    def _():
        pltpu.make_async_copy(stage, stage, stage_sem).wait()
        for a in range(2):
            pltpu.make_async_remote_copy(
                src_ref=stage.at[a],
                dst_ref=xin.at[a, strip(me), cols(0)],
                send_sem=in_send,
                recv_sem=first_recv.at[0],
                device_id=beside_device,
                device_id_type=MESH,
            ).start()

    scatter(0, first_recv, jnp.where(early, 1, 0))

    def rest(second_recv, chain_recv, t_recv, g_recv, out_send, out_recv,
             p_send, s_send, t_send, g_send, gain_sem, hop_send, hop_recv, own_sem, hold_sem,
             tail_send, tail_recv):
        in_recv = first_recv, second_recv

        def announce(p, carry):
            _, device = place(p)
            pl.semaphore_signal(entered.at[0], inc=1, device_id=device, device_id_type=MESH)
            return carry

        lax.fori_loop(1, peers, announce, 0)
        gains = pltpu.make_async_copy(gain_hbm, gain, gain_sem)
        gains.start()

        if n_inner == 2:
            @pl.when(jnp.logical_not(inside))
            def _():
                pl.semaphore_signal(entered.at[0], inc=1, device_id=across, device_id_type=MESH)

        @pl.when(jnp.logical_not(first))
        def _():
            pl.semaphore_signal(entered.at[0], inc=1, device_id=earlier, device_id_type=MESH)

        @pl.when(first)
        def _():
            def carried_in(c, carry):
                pltpu.make_async_copy(
                    s0_hbm.at[pl.ds(j * heads + c * step, step)], pin.at[piece(c)], chain_recv.at[c],
                ).start()
                return carry

            lax.fori_loop(0, chunks, carried_in, 0)

        @pl.when(last)
        def _():
            sin[...] = jnp.zeros_like(sin)

        row = lax.broadcasted_iota(jnp.int32, (block, block), 0)
        col = lax.broadcasted_iota(jnp.int32, (block, block), 1)
        causal = col <= row
        gains.wait()

        for more_x in range(n_inner):
            for more_z in range(2):
                @pl.when(jnp.logical_and(inner == n_inner - 1 - more_x, last == (more_z == 0)))
                def _(more=more_x + more_z):
                    pl.semaphore_wait(entered.at[0], peers - 1 + more)

        if n_inner == 2:
            @pl.when(inside)
            def _():
                pl.semaphore_signal(entered.at[1], inc=1, device_id=across, device_id_type=MESH)

        @pl.when(jnp.logical_not(last))
        def _():
            pl.semaphore_signal(entered.at[1], inc=1, device_id=later, device_id_type=MESH)

        if detours:
            @pl.when(owes)
            def _():
                pl.semaphore_signal(entered.at[2], inc=1, device_id=partner, device_id_type=MESH)

        scatter(1, second_recv, 0)

        for more_x in range(n_inner):
            for more_z in range(2):
                if more_x + more_z > 0:
                    @pl.when(jnp.logical_and(inner == more_x, first == (more_z == 0)))
                    def _(more=more_x + more_z):
                        pl.semaphore_wait(entered.at[1], more)

        if detours:
            @pl.when(owes)
            def _():
                pl.semaphore_wait(entered.at[2], 1)

        def arrived(phase, c):
            ref = xin.at[pl.ds(2 * phase, 2), :, cols(c)]
            pltpu.make_async_copy(ref, ref, in_recv[phase].at[c]).wait()

        def give(phase, c):
            def back(p, carry):
                other, device = place(p)
                for a in range(2):
                    def send(dst, device, recv, a=a):
                        pltpu.make_async_remote_copy(
                            src_ref=xout.at[2 * phase + a, strip(other), cols(c)], dst_ref=dst,
                            send_sem=out_send, recv_sem=recv, device_id=device, device_id_type=MESH,
                        ).start()

                    target = targets[phase][a].at[:, column(me, c)]
                    if detours and phase == 0 and a < DETOUR_ARRAYS:
                        detour = jnp.logical_and(owes, jnp.logical_and(c < DETOUR_CHUNKS, p == 1))

                        @pl.when(detour)
                        def _():
                            send(hop.at[a, :, cols(c)], hop_device, hop_recv)

                        @pl.when(jnp.logical_not(detour))
                        def _():
                            send(target, device, out_recv)
                    elif late and phase == 1:
                        held = jnp.logical_and(p == 1, c >= chunks - late)

                        @pl.when(held)
                        def _(a=a):
                            at = pl.multiple_of((c - (chunks - late)) * span, span)
                            pltpu.make_async_copy(
                                xout.at[2 + a, strip(other), cols(c)],
                                hold.at[a, :, pl.ds(at, span)], hold_sem).start()

                        @pl.when(jnp.logical_not(held))
                        def _():
                            send(target, device, out_recv)
                    else:
                        send(target, device, out_recv)
                return carry

            lax.fori_loop(1, peers, back, 0)
            for a in range(2):
                pltpu.make_async_copy(
                    xout.at[2 * phase + a, strip(me), cols(c)],
                    targets[phase][a].at[:, column(me, c)],
                    own_sem,
                ).start()

        def state_copy(src, dst, send, recv, c, device):
            return pltpu.make_async_remote_copy(
                src_ref=src.at[piece(c)], dst_ref=dst.at[piece(c)], send_sem=send,
                recv_sem=recv.at[c], device_id=device, device_id_type=MESH)

        def landed(ref, recv, c):
            pltpu.make_async_copy(ref.at[piece(c)], ref.at[piece(c)], recv.at[c]).wait()

        def lanes(c, h):
            return pl.ds(pl.multiple_of(c * span + h * HEAD_DIM, HEAD_DIM), HEAD_DIM)

        def block_states(c):
            arrived(0, c)
            for h in range(step):
                n, hc = c * step + h, lanes(c, h)
                run = dot(xin[0, :block, hc], xin[1, :block, hc], TN)
                for b in range(1, sub):
                    r = slice(b * block, (b + 1) * block)
                    cum[n, b - 1] = run
                    run = run + dot(xin[0, r, hc], xin[1, r, hc], TN)
                tot[n] = run
            if n_inner == 2:
                state_copy(tot, xt, t_send, t_recv, c, across).start()

        def pass_prefix(c):
            if n_inner == 2:
                landed(xt, t_recv, c)
            landed(pin, chain_recv, c)

            @pl.when(jnp.logical_not(last))
            def _():
                for h in range(step):
                    n = c * step + h
                    psend[n] = pin[n] + tot[n] + xt[n] if n_inner == 2 else pin[n] + tot[n]
                state_copy(psend, pin, p_send, chain_recv, c, later).start()

            for h in range(step):
                n = c * step + h
                before = pin[n]
                if n_inner == 2:
                    before = before + jnp.where(inner == 1, xt[n], 0.0)
                prefix[n, 0] = before.astype(BF16)
                for b in range(1, sub):
                    prefix[n, b] = (before + cum[n, b - 1]).astype(BF16)

        def attend(c):
            arrived(1, c)
            for h in range(step):
                n, hc = c * step + h, lanes(c, h)
                at = pl.multiple_of((j * heads + n) * HEAD_DIM, HEAD_DIM)
                g = gain[pl.ds(at, HEAD_DIM)].reshape(1, HEAD_DIM)
                run = None
                for b in reversed(range(sub)):
                    r = slice(b * block, (b + 1) * block)
                    k, v, q, up = xin[0, r, hc], xin[1, r, hc], xin[2, r, hc], xin[3, r, hc]
                    state = prefix[n, b]
                    w = jnp.where(causal, dot(q, k, NT), 0.0).astype(BF16)
                    att = dot(w, v, NN) + dot(q, state, NN)
                    inv = lax.rsqrt(jnp.mean(att * att, axis=-1, keepdims=True) + EPSILON)
                    normed = att * inv
                    xout[0, r, hc] = (normed * g).astype(BF16)
                    scaled = up.astype(F32) * g
                    ga = ((scaled - normed * jnp.mean(scaled * normed, axis=-1, keepdims=True))
                          * inv).astype(BF16)
                    gw = jnp.where(causal, dot(ga, v, NT), 0.0).astype(BF16)
                    xout[1, r, hc] = (dot(gw, k, NN) + dot(ga, state, NT)).astype(BF16)
                    part[0, r, hc] = dot(gw, q, TN)
                    part[1, r, hc] = dot(w, ga, TN)
                    if run is not None:
                        gcum[n, b] = run
                    grad = dot(q, ga, TN)
                    run = grad if run is None else run + grad
                gtot[n] = run
            if n_inner == 2:
                state_copy(gtot, xg, g_send, g_recv, c, across).start()
            give(0, c)

        def finish(c):
            if n_inner == 2:
                landed(xg, g_recv, c)

            @pl.when(jnp.logical_not(last))
            def _():
                landed(sin, chain_recv, c)

            @pl.when(jnp.logical_not(first))
            def _():
                for h in range(step):
                    n = c * step + h
                    ssend[n] = sin[n] + gtot[n] + xg[n] if n_inner == 2 else sin[n] + gtot[n]
                state_copy(ssend, sin, s_send, chain_recv, c, earlier).start()

            for h in range(step):
                n, hc = c * step + h, lanes(c, h)
                after = sin[n]
                if n_inner == 2:
                    after = after + jnp.where(inner == 0, xg[n], 0.0)
                for b in range(sub):
                    r = slice(b * block, (b + 1) * block)
                    suffix = (after + gcum[n, b] if b < sub - 1 else after).astype(BF16)
                    xout[2, r, hc] = (part[0, r, hc] + dot(xin[1, r, hc], suffix, NT)).astype(BF16)
                    xout[3, r, hc] = (part[1, r, hc] + dot(xin[0, r, hc], suffix, NN)).astype(BF16)
            give(1, c)

        prefix_lag = jnp.minimum(2 + 2 * outer, chunks)
        suffix_lag = chunks + 2 + 2 * (n_outer - 1 - outer)

        def tick(i, carry):
            @pl.when(i < chunks)
            def _():
                block_states(i)

            @pl.when(jnp.logical_and(i >= prefix_lag, i < prefix_lag + chunks))
            def _():
                pass_prefix(i - prefix_lag)

            @pl.when(jnp.logical_and(i >= chunks, i < 2 * chunks))
            def _():
                attend(i - chunks)

            @pl.when(jnp.logical_and(i >= suffix_lag, i < suffix_lag + chunks))
            def _():
                finish(i - suffix_lag)

            return carry

        lax.fori_loop(0, 2 * chunks + 2 * n_outer, tick, 0)

        if detours:
            @pl.when(relays)
            def _():
                pltpu.make_async_copy(hop, hop, hop_recv).wait()
                first_head = (1 - hd) * (sub * heads) + j * heads
                whole = pl.ds(pl.multiple_of(first_head * HEAD_DIM, span), hop.shape[2])
                for a in range(DETOUR_ARRAYS):
                    pltpu.make_async_remote_copy(
                        src_ref=hop.at[a], dst_ref=targets[0][a].at[:, whole], send_sem=hop_send,
                        recv_sem=out_recv, device_id=passed_to, device_id_type=MESH).start()
                pltpu.make_async_copy(hop, hop, hop_send).wait()

        sent = xin.at[:, pl.ds(0, (peers - 1) * rows)]
        back = xin.at[:, :, pl.ds(0, 5 * chunks // 8 * span)] if late else sent
        mine = xin.at[:, pl.ds(0, rows)]
        if late:
            to_partner = pltpu.make_async_remote_copy(
                src_ref=hold, dst_ref=tail, send_sem=tail_send, recv_sem=tail_recv,
                device_id=partner, device_id_type=MESH)
            pltpu.make_async_copy(hold, hold, hold_sem).wait()

            @pl.when(j == sub - 1)
            def _():
                to_partner.start()

        pltpu.make_async_copy(sent, sent, in_send).wait()
        pltpu.make_async_copy(back, back, out_send).wait()
        pltpu.make_async_copy(mine, mine, own_sem).wait()
        if n_inner == 2:
            pltpu.make_async_copy(tot, tot, t_send).wait()
            pltpu.make_async_copy(gtot, gtot, g_send).wait()

        @pl.when(jnp.logical_not(last))
        def _():
            pltpu.make_async_copy(psend, psend, p_send).wait()

        @pl.when(jnp.logical_not(first))
        def _():
            pltpu.make_async_copy(ssend, ssend, s_send).wait()

        pltpu.make_async_copy(back, back, out_recv).wait()
        if late:
            @pl.when(j == sub - 1)
            def _():
                to_partner.wait()

    one = pltpu.SemaphoreType.DMA
    chain = one((chunks,))
    pl.run_scoped(rest, chain, chain, chain, chain, *[one] * 13)


def land(*refs):
    sources, targets, sem = refs[:4], refs[-5:-1], refs[-1]
    copies = [pltpu.make_async_copy(src, dst, sem) for src, dst in zip(sources, targets)]
    for copy in copies:
        copy.start()
    for copy in copies:
        copy.wait()


def last_pieces(sub, hold, tail, written, out, sem, send, recv):
    seq, hd = lax.axis_index("seq"), lax.axis_index("head")
    partner = (seq, 1 - hd)
    barrier = pltpu.get_barrier_semaphore()

    @pl.when(lax.rem(seq, sub) < sub - 1)
    def _():
        pl.semaphore_signal(barrier, inc=1, device_id=partner, device_id_type=MESH)
        pl.semaphore_wait(barrier, 1)
        copy = pltpu.make_async_remote_copy(
            src_ref=hold, dst_ref=out, send_sem=send, recv_sem=recv,
            device_id=partner, device_id_type=MESH)
        copy.start()
        copy.wait()

    @pl.when(lax.rem(seq, sub) == sub - 1)
    def _():
        copy = pltpu.make_async_copy(tail, out, sem)
        copy.start()
        copy.wait()


def land_last(plan, tail, gk_in, gv_in, gk_out, gv_out, sem):
    n_outer, n_inner, sub, n_head, rows, heads, step, late = plan
    seq, hd = lax.axis_index("seq"), lax.axis_index("head")
    first = (1 - hd) * (sub * heads) + lax.rem(seq, sub) * heads + heads - late * step
    at = pl.ds(pl.multiple_of(first * HEAD_DIM, HEAD_DIM), late * step * HEAD_DIM)
    copies = [pltpu.make_async_copy(tail.at[a], out.at[:, at], sem)
              for a, out in enumerate((gk_out, gv_out))]
    for copy in copies:
        copy.start()
    for copy in copies:
        copy.wait()


def per_device(mesh, query, key, value, cotangent, gain, incoming_state):
    n_seq, n_head = mesh.shape["seq"], mesh.shape["head"]
    rows, features = query.shape
    local_heads = incoming_state.shape[0]
    sub = 2 if n_seq % 2 == 0 and local_heads % 2 == 0 else 1
    n_inner = 2 if n_seq % (2 * sub) == 0 else 1
    n_outer = n_seq // (sub * n_inner)
    heads = local_heads // sub
    step = next(s for s in range(max(1, heads // 8), heads + 1) if heads % s == 0)
    chunks = heads // step
    tokens = rows * n_head * sub
    width = heads * HEAD_DIM
    splits = sub == 2 and n_head == 2 and n_inner == 2 and n_outer > 1 and chunks % 8 == 0
    late = chunks if splits else 0
    plan = (n_outer, n_inner, sub, n_head, rows, heads, step, late)
    anywhere = pl.BlockSpec(memory_space=pl.ANY)
    resident = pl.BlockSpec(memory_space=pltpu.HBM)
    state = pltpu.VMEM((heads, HEAD_DIM, HEAD_DIM), F32)
    states = pltpu.VMEM((heads, max(1, sub - 1), HEAD_DIM, HEAD_DIM), F32)
    shapes = [jax.ShapeDtypeStruct((rows, features), BF16)] * 4
    pieces = [jax.ShapeDtypeStruct((2, rows, max(1, late) * step * HEAD_DIM), BF16)] * 2
    *results, hold, tail = pl.pallas_call(
        functools.partial(kernel, plan),
        out_shape=shapes + pieces,
        in_specs=[resident] * 6,
        out_specs=[anywhere] * 6,
        scratch_shapes=[
            pltpu.VMEM((4, tokens, width), BF16),
            pltpu.VMEM((4, tokens, width), BF16),
            pltpu.VMEM((2, tokens, width), F32),
            states, states,
            pltpu.VMEM((heads, sub, HEAD_DIM, HEAD_DIM), BF16),
            state, state, state, state, state, state, state, state,
            pltpu.VMEM((local_heads * HEAD_DIM,), F32),
            pltpu.VMEM((DETOUR_ARRAYS, rows, DETOUR_CHUNKS * step * HEAD_DIM), BF16),
            pltpu.VMEM((2, rows, step * HEAD_DIM), BF16),
            pltpu.SemaphoreType.DMA((chunks,)), pltpu.SemaphoreType.DMA, pltpu.SemaphoreType.DMA,
            pltpu.SemaphoreType.REGULAR((3,)),
        ],
        compiler_params=pltpu.CompilerParams(
            collective_id=0, has_side_effects=True, vmem_limit_bytes=VMEM),
    )(*(pltpu.with_memory_space_constraint(x, pltpu.HBM)
        for x in (query, key, value, cotangent, gain, incoming_state)))
    small = pltpu.CompilerParams(vmem_limit_bytes=1024 * 1024)
    written = pl.pallas_call(
        land,
        out_shape=shapes,
        in_specs=[anywhere] * 4,
        out_specs=[anywhere] * 4,
        scratch_shapes=[pltpu.SemaphoreType.DMA],
        compiler_params=small,
    )(*results)
    if not late:
        return tuple(written)
    output, grad_query, grad_key, grad_value = written
    tail = pl.pallas_call(
        functools.partial(last_pieces, sub),
        out_shape=pieces[0],
        in_specs=[anywhere] * 3,
        out_specs=anywhere,
        scratch_shapes=[pltpu.SemaphoreType.DMA] * 3,
        compiler_params=pltpu.CompilerParams(
            collective_id=1, has_side_effects=True, vmem_limit_bytes=1024 * 1024),
    )(hold, tail, pltpu.with_memory_space_constraint(grad_key, pltpu.HBM))
    grad_key, grad_value = pl.pallas_call(
        functools.partial(land_last, plan),
        out_shape=shapes[:2],
        in_specs=[anywhere] * 3,
        out_specs=[anywhere] * 2,
        input_output_aliases={1: 0, 2: 1},
        scratch_shapes=[pltpu.SemaphoreType.DMA],
        compiler_params=small,
    )(tail, grad_key, grad_value)
    return output, grad_query, grad_key, grad_value


def solution(mesh):
    tokens = P(("seq", "head"), None)
    return jax.shard_map(
        functools.partial(per_device, mesh),
        mesh=mesh,
        in_specs=(tokens, tokens, tokens, tokens, P("head"), P("head", None, None)),
        out_specs=(tokens, tokens, tokens, tokens),
        check_vma=False,
    )
```
